128 devices in a mesh: rows: 8 (over y, core), feat: 16 (over z, x).
Axes of the slice: x: 4, y: 4, z: 4, core: 2. Of those that a mesh axis runs over, the one named last changes fastest.
Arguments:
- margins: float32 [24576, 32], P(('rows', 'feat')), may hold values from -30 to 260
- labels: int32 [24576], P(('rows', 'feat')), may hold values from 0 to 31
- row_bins: int32 [1024, 24576], P('feat', 'rows'), may hold values from 0 to 63
- parents: int32 [24576], P('rows'), may hold values from 0 to 7
- split_feature: int32 [8], replicated, may hold values from 0 to 1023
- split_bin: int32 [8], replicated, may hold values from 16 to 47
- leaf_values: float32 [16, 32], replicated, may hold values from -4 to 4
Outputs:
- split_gains: float32 [16, 1024, 64], P('rows', 'feat')
- node_totals: float32 [16, 64], replicated
The draws below stay inside these ranges and needn't reach their ends.
All inputs are finite; a program needn't handle non-finite values.
Results may differ from the reference program's by a relative error of at most 0.0017.
Values may be sent and summed in bfloat16 or wider, within the bound.
A program may use at most 64 MiB of HBM per device.

```python
import math
import jax
import jax.numpy as jnp
import numpy as np
from jax import lax

C = 32
F = 1024
BINS = 64
NODES = 16
PARENTS = 8
TOTAL_ROWS = 24576


def draw_margins(key, part):
    first_key = jax.random.fold_in(key, 0)
    base = jnp.clip(jax.random.normal(first_key, (TOTAL_ROWS, C), jnp.float32), -8.0, 8.0)
    row_ids = jnp.arange(TOTAL_ROWS, dtype=jnp.int32)
    column_ids = jnp.arange(C, dtype=jnp.int32)
    position = row_ids.astype(jnp.float32) / TOTAL_ROWS
    base = base + jnp.where(column_ids[None, :] == 0, 3.0 * position[:, None], 0.0)
    return base


def with_ends(result, key, least, largest):
    place = [jax.random.randint(jax.random.fold_in(key, axis), (), 0, length) for axis, length in enumerate(result.shape)]
    main_axis = result.shape.index(max(result.shape))
    beside = place[:main_axis] + [(place[main_axis] + 1) % result.shape[main_axis]] + place[main_axis + 1:]
    return result.at[tuple(place)].set(least).at[tuple(beside)].set(largest)


def rank_table(count, lean):
    loads = [(1 << 20) // math.isqrt(rank ** lean) + 1 for rank in range(1, count + 1)]
    deviation = 1 + sum(loads) // (1 << 30)
    return np.cumsum(np.array([max(1, weight // deviation) for weight in loads]))


def ranked_ids(key, shape, amount, slope):
    grid = rank_table(amount, slope)
    pick = jax.random.randint(jax.random.fold_in(key, 1), shape, 0, int(grid[amount - 1]))
    rank = jnp.searchsorted(jnp.asarray(grid, jnp.int32), pick, side="right")
    return jax.random.permutation(jax.random.fold_in(key, 2), amount)[rank].astype(jnp.int32)


def normal_values(own_key, dims, scale, reach, held_as=jnp.bfloat16):
    result = jax.random.normal(own_key, dims, jnp.float32) * scale
    return jnp.minimum(jnp.maximum(result, -reach), reach).astype(held_as)


def setup_inputs(seed: int = 0) -> dict:
    arg_keys = jax.random.split(jax.random.key(seed), 8)
    return {
        "margins": draw_margins(jax.random.fold_in(arg_keys[7], 71), 0),
        "labels": with_ends(jax.random.randint(arg_keys[1], (TOTAL_ROWS,), 0, C), jax.random.fold_in(arg_keys[1], 1), 0, C - 1).astype(jnp.int32),
        "row_bins": with_ends(jax.random.randint(arg_keys[2], (F, TOTAL_ROWS), 0, BINS), jax.random.fold_in(arg_keys[2], 1), 0, BINS - 1).astype(jnp.int32),
        "parents": with_ends(ranked_ids(arg_keys[3], (TOTAL_ROWS,), PARENTS, 2), jax.random.fold_in(arg_keys[3], 3), 0, PARENTS - 1).astype(jnp.int32),
        "split_feature": with_ends(jax.random.randint(arg_keys[4], (PARENTS,), 0, F), jax.random.fold_in(arg_keys[4], 1), 0, F - 1).astype(jnp.int32),
        "split_bin": with_ends(jax.random.randint(arg_keys[5], (PARENTS,), BINS // 4, 3 * BINS // 4), jax.random.fold_in(arg_keys[5], 1), BINS // 4, (3 * BINS // 4) - 1).astype(jnp.int32),
        "leaf_values": normal_values(arg_keys[6], (NODES, C), 1.0, 4.0, jnp.float32),
    }


hess_ridge = 1.0


def gain_scores(left_sums, totals, classes):
    grad_left = left_sums[..., :classes]
    hess_left = left_sums[..., classes:]
    grad_whole = totals[..., :classes]
    hess_whole = totals[..., classes:]
    grad_right = grad_whole - grad_left
    hess_right = hess_whole - hess_left
    score = grad_left * grad_left / (hess_left + hess_ridge) + grad_right * grad_right / (hess_right + hess_ridge) - grad_whole * grad_whole / (hess_whole + hess_ridge)
    return jnp.mean(score, axis=-1)


def reference(margins, labels, row_bins, parents, split_feature, split_bin, leaf_values):
    chosen = jnp.take_along_axis(row_bins, split_feature[parents][None, :], axis=0)[0]
    node_ids = 2 * parents + (chosen > split_bin[parents]).astype(jnp.int32)
    logits = margins + leaf_values[node_ids]
    probabilities = jax.nn.softmax(logits, axis=1)
    label_hot = (labels[:, None] == jnp.arange(C, dtype=jnp.int32)[None, :]).astype(jnp.float32)
    gradient = probabilities - label_hot
    hessian = 2.0 * probabilities * (1.0 - probabilities)
    grad_hess = jnp.concatenate([gradient, hessian], axis=1).astype(jnp.bfloat16).astype(jnp.float32)
    node_totals = jax.ops.segment_sum(grad_hess, node_ids, num_segments=NODES)

    def feature_hist(column):
        keys = node_ids * BINS + column
        summed = jax.ops.segment_sum(grad_hess, keys, num_segments=NODES * BINS)
        return summed.reshape(NODES, BINS, 2 * C)

    histogram = lax.map(feature_hist, row_bins)
    left_sums = jnp.cumsum(histogram, axis=2)
    scores = gain_scores(left_sums, node_totals[None, :, None, :], C)
    return jnp.transpose(scores, (1, 0, 2)), node_totals
```

```python
import functools

import jax
import jax.numpy as jnp
from jax import lax
from jax.experimental import pallas as pl
from jax.experimental.pallas import tpu as pltpu
from jax.sharding import PartitionSpec as P

MESH = pl.DeviceIdType.MESH
BINS = 64
NODES = 16
CLASSES = 32
COLS = 2 * CLASSES
PARENTS = 8
RIDGE = 1.0
LANES = 128
NR = 8
NF = 16
OWN = 192
GROUP = 3072
KB = GROUP // LANES
FD = 64
FL = FD // NR
UNIT = 12 * LANES
BF = jnp.bfloat16
F32 = jnp.float32


def own_gradients(margins, labels, parents, leaf_t, side):
    leaf = jnp.zeros(margins.shape, F32)
    for p in range(PARENTS):
        column = leaf_t[:, 2 * p + side : 2 * p + side + 1]
        leaf = jnp.where(parents == p, column, leaf)
    logits = margins + leaf
    top = jnp.max(logits, axis=0, keepdims=True)
    grown = jnp.exp(logits - top)
    prob = grown / jnp.sum(grown, axis=0, keepdims=True)
    classes = lax.broadcasted_iota(jnp.int32, margins.shape, 0)
    hot = jnp.where(classes == labels, 1.0, 0.0)
    return prob - hot, 2.0 * prob * (1.0 - prob)


def kernel(
    sf_ref, sb_ref, margin_ref, label_ref, bins_ref, par_ref, parrow_ref, leaf_ref,
    gain_ref, total_ref,
    bit_f32, bit_send, bit_recv, bin_send, bin_recv, bin_all, node_all,
    grads, weighted, mask, acc, unit_tot, gain_send, gain_recv,
    bit_ss, bit_rs, bin_ss, bin_rs, node_ss, node_rs, y_ss, y_rs, x_ss, x_rs,
    z_ss, z_rs, sib_ss, sib_rs, out_ss, out_rs,
):
    row = lax.axis_index("rows")
    feat = lax.axis_index("feat")
    y, core = row // 2, row % 2
    z, x = feat // 4, feat % 4
    odd = feat % 2
    xo = x // 2

    def send(src, dst, ss, rs, r, f):
        return pltpu.make_async_remote_copy(
            src_ref=src, dst_ref=dst, send_sem=ss, recv_sem=rs,
            device_id=(r, f), device_id_type=MESH,
        )

    barrier = pltpu.get_barrier_semaphore()
    for d in range(1, NF):
        pl.semaphore_signal(barrier, inc=1, device_id=(row, (feat + d) % NF), device_id_type=MESH)
    for d in range(1, NR):
        pl.semaphore_signal(barrier, inc=1, device_id=((row + d) % NR, feat), device_id_type=MESH)

    right = jnp.zeros((1, GROUP), F32)
    for p in range(PARENTS):
        local = sf_ref[p] - feat * FD
        owned = jnp.logical_and(local >= 0, local < FD).astype(jnp.int32)
        at = jnp.minimum(jnp.maximum(local, 0), FD - 1)
        limit = sb_ref[p] * owned + BINS * (1 - owned)
        hit = jnp.logical_and(bins_ref[pl.ds(at, 1), :] > limit, parrow_ref[...] == p)
        right = jnp.where(hit, 1.0, right)
    bit_f32[...] = jnp.zeros_like(bit_f32)
    for k in range(KB):
        bit_f32[k : k + 1, :] = right[:, k * LANES : (k + 1) * LANES]
    bit_send[...] = bit_f32[...].astype(BF)

    pl.semaphore_wait(barrier, NF - 1 + NR - 1)

    def bit_copy(d):
        return send(
            bit_send, bit_recv.at[d], bit_ss.at[d], bit_rs.at[d], row, (feat + d) % NF
        )

    for d in range(1, NF):
        bit_copy(d).start()

    def bin_copy(d):
        to = (row + d) % NR
        return send(bin_send.at[d], bin_recv.at[d], bin_ss.at[d], bin_rs.at[d], to, feat)

    def load_bins(to):
        first = pl.multiple_of(to * FL, FL)
        parts = [
            bins_ref[pl.ds(first, FL), k * LANES : (k + 1) * LANES].astype(F32)
            for k in range(KB)
        ]
        return parts

    for d in range(1, NR):
        parts = load_bins((row + d) % NR)
        bin_send[d] = jnp.concatenate(parts, axis=0).astype(BF)
        bin_copy(d).start()
    for k, part in enumerate(load_bins(row)):
        bin_all[row, k] = part

    pair = feat // 2

    def arrange(value):
        padded = jnp.concatenate(
            [value, jnp.zeros((value.shape[0], 2 * LANES - OWN), value.dtype)], axis=1
        )
        turned = jnp.concatenate(
            [padded[:, 64:], padded[:, :64]], axis=1
        )
        return jnp.where(odd == 1, turned, padded)

    def own_rows(ref):
        main = ref[pl.ds(3 * pair + 2 * odd, 1), :]
        rest = ref[pl.ds(3 * pair + 1, 1), :]
        return jnp.concatenate([main, rest], axis=1)

    margins = arrange(margin_ref[...])
    labels = arrange(label_ref[...])
    own_parents = own_rows(par_ref)
    leaf_t = leaf_ref[...].T
    left_g, left_h = own_gradients(margins, labels, own_parents, leaf_t, 0)
    right_g, right_h = own_gradients(margins, labels, own_parents, leaf_t, 1)

    bits = bit_send[...].astype(F32)
    for d in range(1, NF):
        bit_copy(d).wait_recv()
        bits = bits + bit_recv[d].astype(F32)
    node_all[row] = (2 * par_ref[...]).astype(F32) + bits[:KB]
    bit_f32[...] = bits

    def node_copy(d):
        to = (row + d) % NR
        return send(node_all.at[row], node_all.at[row], node_ss.at[d], node_rs.at[d], to, feat)

    goes_right = own_rows(bit_f32) > 0.5
    g = jnp.where(goes_right, right_g, left_g)
    h = jnp.where(goes_right, right_h, left_h)
    lane = lax.broadcasted_iota(jnp.int32, (CLASSES, LANES), 1)
    first_half = lane < 64
    keep = first_half == (odd == 0)
    rest = jnp.where(keep, g[:, LANES:], pltpu.roll(h[:, LANES:], 64, 1))
    grads[core, z, x, y] = jnp.concatenate(
        [g[:, :LANES], h[:, :LANES], rest], axis=0
    ).astype(BF)

    def y_copy(d):
        to = ((y + d) % 4) * 2 + core
        at = grads.at[core, z, x, y]
        return send(at, at, y_ss.at[d], y_rs.at[d], to, feat)

    for d in range(1, 4):
        y_copy(d).start()
    for d in range(1, NR):
        node_copy(d).start()

    def x_copy(d):
        at = grads.at[core, z, x]
        return send(at, at, x_ss.at[d], x_rs.at[d], row, 4 * z + (x + d) % 4)

    def x_wait(d):
        at = grads.at[core, z, (x + 4 - d) % 4]
        send(at, at, x_ss.at[d], x_rs.at[d], row, feat).wait_recv()

    def unit_at(half, dz, q):
        return grads.at[half, (z + dz) % 4, pl.ds(2 * ((xo + q) % 2), 2)]

    def z_copy(way, q):
        at = unit_at(core, 0, q)
        to = 4 * ((z + 1 + 2 * way) % 4) + x
        return send(at, at, z_ss.at[way, q], z_rs.at[way, q], row, to)

    def z_wait(way, q):
        at = unit_at(core, 3 - 2 * way, q)
        send(at, at, z_ss.at[way, q], z_rs.at[way, q], row, feat).wait_recv()

    def far_copy(q):
        at = unit_at(core, 3 - 2 * q, q)
        to = 4 * ((z + 1 + 2 * q) % 4) + x
        return send(at, at, z_ss.at[2, q], z_rs.at[2, q], row, to)

    def far_wait(q):
        at = unit_at(core, 2, q)
        send(at, at, z_ss.at[2, q], z_rs.at[2, q], row, feat).wait_recv()

    def sib_copy(dz, q):
        at = unit_at(core, dz, q)
        return send(at, at, sib_ss.at[dz, q], sib_rs.at[dz, q], row + 1 - 2 * core, feat)

    def sib_wait(dz, q):
        at = unit_at(1 - core, dz, q)
        send(at, at, sib_ss.at[dz, q], sib_rs.at[dz, q], row, feat).wait_recv()

    for d in range(1, 4):
        at = grads.at[core, z, x, (y + 4 - d) % 4]
        send(at, at, y_ss.at[d], y_rs.at[d], row, feat).wait_recv()
    for d in (1, 3, 2):
        x_copy(d).start()

    acc[...] = jnp.zeros_like(acc)

    for d in range(1, NR):
        bin_copy(d).wait_recv()
        came = (row + NR - d) % NR
        block = bin_recv[d].astype(F32)
        for k in range(KB):
            bin_all[came, k] = block[k * FL : (k + 1) * FL]
    for d in range(1, NR):
        at = node_all.at[(row + NR - d) % NR]
        send(at, at, node_ss.at[d], node_rs.at[d], row, feat).wait_recv()

    @pl.when(odd == 1)
    def _():
        x_wait(1)

    @pl.when(odd == 0)
    def _():
        x_wait(3)

    z_copy(0, 0).start()
    z_copy(1, 0).start()
    sib_copy(0, 0).start()

    lane_low = lax.broadcasted_iota(jnp.int32, (32, LANES), 1) < 64
    bin_ids = lax.broadcasted_iota(jnp.int32, (BINS, LANES), 0).astype(F32).astype(BF)
    node_ids = lax.broadcasted_iota(jnp.int32, (NODES, LANES), 0).astype(F32).astype(BF)

    def unit(u, carry):
        t, rel = u // 2, u % 2
        group, r = t // 2, t % 2
        mid = ((group + 1) // 2) % 2
        q = (1 - mid) * r + mid * (group - 1)
        dz = mid * (3 - 2 * r) + (1 - mid) * 2 * (group // 3)
        half = (core + rel) % 2

        @pl.when(u == 1)
        def _():
            @pl.when(odd == 1)
            def _():
                x_wait(3)

            @pl.when(odd == 0)
            def _():
                x_wait(1)

            x_wait(2)
            z_copy(0, 1).start()
            z_copy(1, 1).start()
            sib_copy(0, 1).start()
            sib_wait(0, 0)

        @pl.when(u == 3)
        def _():
            sib_wait(0, 1)

        @pl.when(u == 4)
        def _():
            z_wait(0, 0)
            far_copy(0).start()
            sib_copy(3, 0).start()
            z_wait(1, 0)
            sib_copy(1, 0).start()

        @pl.when(u == 5)
        def _():
            sib_wait(3, 0)

        @pl.when(u == 6)
        def _():
            z_wait(1, 1)
            far_copy(1).start()
            sib_copy(1, 1).start()
            z_wait(0, 1)
            sib_copy(3, 1).start()

        @pl.when(u == 7)
        def _():
            sib_wait(1, 0)

        @pl.when(u == 9)
        def _():
            sib_wait(3, 1)

        @pl.when(u == 10)
        def _():
            far_wait(0)
            sib_copy(2, 0).start()
            far_wait(1)
            sib_copy(2, 1).start()

        @pl.when(u == 11)
        def _():
            sib_wait(1, 1)

        @pl.when(u == 13)
        def _():
            sib_wait(2, 0)

        @pl.when(u == 15)
        def _():
            sib_wait(2, 1)

        zz = (z + dz) % 4
        xp = (xo + q) % 2
        first = 3 * (2 * zz + xp)
        hots = []
        pieces = []
        for yy in range(4):
            group_row = 2 * yy + half
            even = grads[half, zz, 2 * xp, yy]
            last = grads[half, zz, 2 * xp + 1, yy]
            rest_e, rest_o = even[64:], last[64:]
            low = jnp.where(lane_low, rest_e, rest_o)
            high = jnp.where(lane_low, rest_o, rest_e).astype(F32)
            high = pltpu.roll(high, 64, 1).astype(BF)
            middle = jnp.concatenate([low, high], axis=0)
            for i, piece in enumerate((even[:64], middle, last[:64])):
                at = (yy * 3 + i) * LANES
                nodes = node_all[group_row, pl.ds(first + i, 1), :].astype(BF)
                nodes_g = jnp.broadcast_to(nodes, (COLS, LANES))
                for n in range(NODES):
                    weighted[n * COLS : (n + 1) * COLS, at : at + LANES] = jnp.where(
                        nodes_g == BF(n), piece, jnp.zeros_like(piece)
                    )
                hots.append(
                    jnp.where(
                        jnp.broadcast_to(nodes, (NODES, LANES)) == node_ids, BF(1), BF(0)
                    )
                )
                pieces.append(piece)
                for f in range(FL):
                    here = bin_all[group_row, first + i, f : f + 1, :].astype(BF)
                    mask[f * BINS : (f + 1) * BINS, at : at + LANES] = jnp.where(
                        jnp.broadcast_to(here, (BINS, LANES)) <= bin_ids, BF(1), BF(0)
                    )
        contract = (((1,), (1,)), ((), ()))
        acc[...] += lax.dot_general(
            weighted[...], mask[...], contract, preferred_element_type=F32
        )
        unit_tot[half * 8 + 2 * zz + xp] = lax.dot_general(
            jnp.concatenate(hots, axis=1),
            jnp.concatenate(pieces, axis=1),
            contract,
            preferred_element_type=F32,
        )
        return carry

    lax.fori_loop(0, 16, unit, 0)

    totals = unit_tot[0]
    for u in range(1, 16):
        totals = totals + unit_tot[u]
    total_ref[...] = totals

    for n in range(NODES):
        base = n * COLS
        gl = acc[base : base + CLASSES, :]
        hl = acc[base + CLASSES : base + COLS, :]
        whole_g = acc[base : base + CLASSES, BINS - 1 : BINS]
        whole_h = acc[base + CLASSES : base + COLS, BINS - 1 : BINS]
        gr = whole_g - gl
        hr = whole_h - hl
        score = (
            gl * gl / (hl + RIDGE)
            + gr * gr / (hr + RIDGE)
            - whole_g * whole_g / (whole_h + RIDGE)
        )
        gain = jnp.sum(score, axis=0, keepdims=True) * (1.0 / CLASSES)
        for k in range(4):
            gain_send[n // 2, (n % 2) * 4 + k : (n % 2) * 4 + k + 1, :] = gain[
                :, k * LANES : (k + 1) * LANES
            ]

    def out_copy(d):
        to = (row + d) % NR
        return send(
            gain_send.at[to], gain_recv.at[row], out_ss.at[d], out_rs.at[d], to, feat
        )

    for d in range(1, NR):
        out_copy(d).start()
    gain_ref[row] = gain_send[row]
    for d in range(1, NR):
        came = (row + NR - d) % NR
        at = gain_recv.at[came]
        send(at, at, out_ss.at[d], out_rs.at[d], row, feat).wait_recv()
        gain_ref[came] = gain_recv[came]

    for d in range(1, NF):
        bit_copy(d).wait_send()
    for d in range(1, NR):
        bin_copy(d).wait_send()
        node_copy(d).wait_send()
        out_copy(d).wait_send()
    for d in range(1, 4):
        y_copy(d).wait_send()
        x_copy(d).wait_send()
    for q in range(2):
        for way in range(2):
            z_copy(way, q).wait_send()
        far_copy(q).wait_send()
        for dz in range(4):
            sib_copy(dz, q).wait_send()


def body(margins, labels, row_bins, parents, split_feature, split_bin, leaf_values):
    vmem = pl.BlockSpec(memory_space=pltpu.VMEM)
    smem = pl.BlockSpec(memory_space=pltpu.SMEM)
    dma = pltpu.SemaphoreType.DMA
    gains, totals = pl.pallas_call(
        kernel,
        out_shape=(
            jax.ShapeDtypeStruct((NR, 8, LANES), F32),
            jax.ShapeDtypeStruct((NODES, COLS), F32),
        ),
        in_specs=[smem, smem] + [vmem] * 6,
        out_specs=(vmem, vmem),
        scratch_shapes=[
            pltpu.VMEM((32, LANES), F32),
            pltpu.VMEM((32, LANES), BF),
            pltpu.VMEM((NF, 32, LANES), BF),
            pltpu.VMEM((NR, KB * FL, LANES), BF),
            pltpu.VMEM((NR, KB * FL, LANES), BF),
            pltpu.VMEM((NR, KB, FL, LANES), F32),
            pltpu.VMEM((NR, KB, LANES), F32),
            pltpu.VMEM((2, 4, 4, 4, 96, LANES), BF),
            pltpu.VMEM((NODES * COLS, UNIT), BF),
            pltpu.VMEM((FL * BINS, UNIT), BF),
            pltpu.VMEM((NODES * COLS, FL * BINS), F32),
            pltpu.VMEM((16, NODES, COLS), F32),
            pltpu.VMEM((NR, 8, LANES), F32),
            pltpu.VMEM((NR, 8, LANES), F32),
            dma((NF,)), dma((NF,)), dma((NR,)), dma((NR,)), dma((NR,)), dma((NR,)),
            dma((4,)), dma((4,)), dma((4,)), dma((4,)),
            dma((3, 2)), dma((3, 2)), dma((4, 2)), dma((4, 2)),
            dma((NR,)), dma((NR,)),
        ],
        compiler_params=pltpu.CompilerParams(
            collective_id=0, has_side_effects=True, vmem_limit_bytes=48 << 20
        ),
    )(
        split_feature,
        split_bin,
        margins.T,
        labels.reshape(1, OWN),
        row_bins,
        parents.reshape(KB, LANES),
        parents.reshape(1, GROUP),
        leaf_values,
    )
    shaped = gains.reshape(NR, 2, 4, 2, BINS).transpose(1, 0, 2, 3, 4)
    return shaped.reshape(2, FD, BINS), totals


def solution(mesh):
    return jax.shard_map(
        body,
        mesh=mesh,
        in_specs=(
            P(("rows", "feat"), None),
            P(("rows", "feat")),
            P("feat", "rows"),
            P("rows"),
            P(),
            P(),
            P(),
        ),
        out_specs=(P("rows", "feat", None), P()),
        check_vma=False,
    )
```

```python
import jax
import jax.numpy as jnp
from jax import lax
from jax.experimental import pallas as pl
from jax.experimental.pallas import tpu as pltpu
from jax.sharding import PartitionSpec as P

MESH = pl.DeviceIdType.MESH
BINS = 64
NODES = 16
CLASSES = 32
COLS = 2 * CLASSES
PARENTS = 8
RIDGE = 1.0
LANES = 128
NR = 8
NF = 16
OWN = 192
GROUP = 3072
KB = GROUP // LANES
FD = 64
FL = FD // NR
FAR_FIRST = (10, 6, 14, 9, 11, 8, 2, 5, 7, 13, 15, 4, 12, 1, 3)
BF = jnp.bfloat16
F32 = jnp.float32


def own_gradients(margins, labels, parents, leaf_t, side):
    leaf = jnp.zeros(margins.shape, F32)
    for p in range(PARENTS):
        column = leaf_t[:, 2 * p + side : 2 * p + side + 1]
        leaf = jnp.where(parents == p, column, leaf)
    logits = margins + leaf
    top = jnp.max(logits, axis=0, keepdims=True)
    grown = jnp.exp(logits - top)
    prob = grown / jnp.sum(grown, axis=0, keepdims=True)
    classes = lax.broadcasted_iota(jnp.int32, margins.shape, 0)
    hot = jnp.where(classes == labels, 1.0, 0.0)
    return prob - hot, 2.0 * prob * (1.0 - prob)


def kernel(
    sf_hbm, sb_hbm, margin_hbm, label_hbm, bins_hbm, par_hbm, parrow_hbm, leaf_hbm,
    gain_ref, total_ref,
    sf_ref, sb_ref, margin_ref, label_ref, bins_ref, par_ref, parrow_ref, leaf_ref,
    bit_f32, bit_send, bit_recv, bin_send, bin_recv, bin_all, node_all,
    spec, grads, acc, unit_tot, gain_send, gain_recv,
    in_sem, bit_ss, bit_rs, bin_ss, bin_rs, node_ss, node_rs, x_ss, x_rs,
    y_ss, y_rs, z_ss, z_rs, far_ss, far_rs, sib_ss, sib_rs, out_ss, out_rs,
):
    row = lax.axis_index("rows")
    feat = lax.axis_index("feat")
    y, core = row // 2, row % 2
    z, x = feat // 4, feat % 4
    odd = feat % 2

    inputs = [
        pltpu.make_async_copy(src, dst, in_sem.at[k])
        for k, (src, dst) in enumerate((
            (bins_hbm, bins_ref), (parrow_hbm, parrow_ref), (sf_hbm, sf_ref),
            (sb_hbm, sb_ref), (margin_hbm, margin_ref), (label_hbm, label_ref),
            (par_hbm, par_ref), (leaf_hbm, leaf_ref),
        ))
    ]
    for copy in inputs:
        copy.start()

    def send(src, dst, ss, rs, r, f):
        return pltpu.make_async_remote_copy(
            src_ref=src, dst_ref=dst, send_sem=ss, recv_sem=rs,
            device_id=(r, f), device_id_type=MESH,
        )

    barrier = pltpu.get_barrier_semaphore()
    for d in FAR_FIRST:
        pl.semaphore_signal(barrier, inc=1, device_id=(row, (feat + d) % NF), device_id_type=MESH)
    for d in range(1, NR):
        pl.semaphore_signal(barrier, inc=1, device_id=((row + d) % NR, feat), device_id_type=MESH)

    for copy in inputs:
        copy.wait()

    right = jnp.zeros((1, GROUP), F32)
    for p in range(PARENTS):
        local = sf_ref[p] - feat * FD
        owned = jnp.logical_and(local >= 0, local < FD).astype(jnp.int32)
        at = jnp.minimum(jnp.maximum(local, 0), FD - 1)
        limit = sb_ref[p] * owned + BINS * (1 - owned)
        hit = jnp.logical_and(bins_ref[pl.ds(at, 1), :] > limit, parrow_ref[...] == p)
        right = jnp.where(hit, 1.0, right)
    bit_f32[...] = jnp.zeros_like(bit_f32)
    for k in range(KB):
        bit_f32[k : k + 1, :] = right[:, k * LANES : (k + 1) * LANES]
    bit_send[...] = bit_f32[...].astype(BF)

    def arrange(value):
        padded = jnp.concatenate(
            [value, jnp.zeros((value.shape[0], 2 * LANES - OWN), value.dtype)], axis=1
        )
        turned = jnp.concatenate([padded[:, 64:], padded[:, :64]], axis=1)
        return jnp.where(odd == 1, turned, padded)

    def rows_of(ref, pair, side):
        main = ref[pl.ds(3 * pair + 2 * side, 1), :]
        rest = ref[pl.ds(3 * pair + 1, 1), :]
        return main, rest

    margins = arrange(margin_ref[...])
    labels = arrange(label_ref[...])
    own_parents = jnp.concatenate(rows_of(par_ref, feat // 2, odd), axis=1)
    leaf_t = leaf_ref[...].T
    first_half = lax.broadcasted_iota(jnp.int32, (CLASSES, LANES), 1) < 64
    keep = first_half == (odd == 0)
    for side in range(2):
        g, h = own_gradients(margins, labels, own_parents, leaf_t, side)
        rest = jnp.where(keep, g[:, LANES:], pltpu.roll(h[:, LANES:], 64, 1))
        spec[x, side] = jnp.concatenate([g[:, :LANES], h[:, :LANES], rest], axis=0).astype(BF)

    def load_bins(to):
        first = pl.multiple_of(to * FL, FL)
        return [
            bins_ref[pl.ds(first, FL), k * LANES : (k + 1) * LANES].astype(F32)
            for k in range(KB)
        ]

    for d in range(1, NR):
        bin_send[d] = jnp.concatenate(load_bins((row + d) % NR), axis=0).astype(BF)
    for k, part in enumerate(load_bins(row)):
        bin_all[row, k] = part

    def bit_copy(d):
        return send(
            bit_send, bit_recv.at[d], bit_ss.at[d], bit_rs.at[d], row, (feat + d) % NF
        )

    def x_copy(d):
        at = spec.at[x]
        return send(at, at, x_ss.at[d], x_rs.at[d], row, 4 * z + (x + d) % 4)

    def bin_copy(d):
        to = (row + d) % NR
        return send(bin_send.at[d], bin_recv.at[d], bin_ss.at[d], bin_rs.at[d], to, feat)

    def node_copy(d):
        to = (row + d) % NR
        return send(node_all.at[row], node_all.at[row], node_ss.at[d], node_rs.at[d], to, feat)

    def arrived(at, sem):
        send(at, at, sem, sem, row, feat).wait_recv()

    def order(i):
        return i + i // 2 - 2 * (i // 3)

    def block(half, dz, dy):
        return grads.at[half, (z + dz) % 4, (y + dy) % 4]

    def y_copy(way):
        at = block(core, 0, 0)
        to = 2 * ((y + 1 + 2 * way) % 4) + core
        return send(at, at, y_ss.at[way], y_rs.at[way], to, feat)

    def y_far_copy(way):
        at = block(core, 0, 3 - 2 * way).at[pl.ds(2 * way, 2)]
        to = 2 * ((y + 1 + 2 * way) % 4) + core
        return send(at, at, y_ss.at[2 + way], y_rs.at[2 + way], to, feat)

    def z_copy(way, i):
        at = block(core, 0, order(i))
        to = 4 * ((z + 1 + 2 * way) % 4) + x
        return send(at, at, z_ss.at[way, i], z_rs.at[way, i], row, to)

    def far_copy(i):
        way = i // 2
        at = block(core, 3 - 2 * way, order(i))
        to = 4 * ((z + 1 + 2 * way) % 4) + x
        return send(at, at, far_ss.at[i], far_rs.at[i], row, to)

    def sib_copy(dz, i):
        at = block(core, dz, order(i))
        return send(at, at, sib_ss.at[dz, i], sib_rs.at[dz, i], row + 1 - 2 * core, feat)

    def sib_wait(dz, i):
        arrived(block(1 - core, dz, order(i)), sib_rs.at[dz, i])

    def pass_on(i):
        sib_copy(0, i).start()
        z_copy(0, i).start()
        z_copy(1, i).start()

    def z_arrival(i):
        for way in range(2):
            arrived(block(core, 3 - 2 * way, order(i)), z_rs.at[way, i])
            if i // 2 == way:
                far_copy(i).start()
            sib_copy(3 - 2 * way, i).start()

    def far_arrival(i):
        arrived(block(core, 2, order(i)), far_rs.at[i])
        sib_copy(2, i).start()

    pl.semaphore_wait(barrier, NF - 1 + NR - 1)
    for d in FAR_FIRST:
        bit_copy(d).start()
    for d in (1, 3, 2):
        x_copy(d).start()
    for d in range(1, NR):
        bin_copy(d).start()

    acc[...] = jnp.zeros_like(acc)

    bits = bit_send[...].astype(F32)
    for d in range(1, NF):
        bit_copy(d).wait_recv()
        bits = bits + bit_recv[d].astype(F32)
    node_all[row] = (2 * par_ref[...]).astype(F32) + bits[:KB]
    bit_f32[...] = bits
    for d in range(1, NR):
        node_copy(d).start()

    for d in (1, 3, 2):
        arrived(spec.at[(x + 4 - d) % 4], x_rs.at[d])
    for xx in range(4):
        main, rest = rows_of(bit_f32, 2 * z + xx // 2, xx % 2)
        low = lax.broadcasted_iota(jnp.int32, (1, LANES), 1) < 64
        turned = jnp.concatenate([rest[:, 64:], rest[:, :64]], axis=1)
        rest = jnp.where(low, rest, turned) if xx % 2 == 0 else jnp.where(low, turned, rest)
        side = jnp.concatenate(
            [jnp.broadcast_to(main, (64, LANES)), jnp.broadcast_to(rest, (32, LANES))], axis=0
        ).astype(BF)
        grads[core, z, y, xx] = jnp.where(side > BF(0.5), spec[xx, 1], spec[xx, 0])
    sib_copy(0, 0).start()
    y_copy(0).start()
    y_copy(1).start()
    z_copy(0, 0).start()
    z_copy(1, 0).start()

    for d in range(1, NR):
        bin_copy(d).wait_recv()
        came = (row + NR - d) % NR
        part = bin_recv[d].astype(F32)
        for k in range(KB):
            bin_all[came, k] = part[k * FL : (k + 1) * FL]
    for d in range(1, NR):
        arrived(node_all.at[(row + NR - d) % NR], node_rs.at[d])

    lane_low = lax.broadcasted_iota(jnp.int32, (32, LANES), 1) < 64
    bin_ids = lax.broadcasted_iota(jnp.int32, (BINS, LANES), 0).astype(F32).astype(BF)
    node_ids = lax.broadcasted_iota(jnp.int32, (NODES, LANES), 0).astype(F32).astype(BF)
    contract = (((1,), (1,)), ((), ()))

    def accumulate(blocks):
        weighted, masks = [], []
        for half, zz, yy in blocks:
            group = 2 * yy + half
            hots, pieces = [], []
            for q in range(2):
                even = grads[half, zz, yy, 2 * q]
                last = grads[half, zz, yy, 2 * q + 1]
                rest_e, rest_o = even[64:], last[64:]
                low = jnp.where(lane_low, rest_e, rest_o)
                high = jnp.where(lane_low, rest_o, rest_e).astype(F32)
                high = pltpu.roll(high, 64, 1).astype(BF)
                middle = jnp.concatenate([low, high], axis=0)
                first = 3 * (2 * zz + q)
                for i, piece in enumerate((even[:64], middle, last[:64])):
                    nodes = node_all[group, pl.ds(first + i, 1), :].astype(BF)
                    wide = jnp.broadcast_to(nodes, (COLS, LANES))
                    zero = jnp.zeros_like(piece)
                    weighted.append(
                        jnp.concatenate(
                            [jnp.where(wide == BF(n), piece, zero) for n in range(NODES)],
                            axis=0,
                        )
                    )
                    same = jnp.broadcast_to(nodes, (NODES, LANES)) == node_ids
                    hots.append(jnp.where(same, BF(1), BF(0)))
                    pieces.append(piece)
                    rows = []
                    for f in range(FL):
                        here = bin_all[group, first + i, f : f + 1, :].astype(BF)
                        under = jnp.broadcast_to(here, (BINS, LANES)) <= bin_ids
                        rows.append(jnp.where(under, BF(1), BF(0)))
                    masks.append(jnp.concatenate(rows, axis=0))
            unit_tot[(half * 4 + zz) * 4 + yy] = lax.dot_general(
                jnp.concatenate(hots, axis=1),
                jnp.concatenate(pieces, axis=1),
                contract,
                preferred_element_type=F32,
            )
        acc[...] += lax.dot_general(
            jnp.concatenate(weighted, axis=1),
            jnp.concatenate(masks, axis=1),
            contract,
            preferred_element_type=F32,
        )

    def near(u, carry):
        @pl.when(u == 0)
        def _():
            sib_wait(0, 0)

        @pl.when(u == 1)
        def _():
            for way in range(2):
                arrived(block(core, 0, 3 - 2 * way), y_rs.at[way])
                y_far_copy(way).start()
            pass_on(1)
            pass_on(2)
            z_arrival(0)

        @pl.when(u == 2)
        def _():
            for way in range(2):
                arrived(block(core, 0, 2).at[pl.ds(2 * way, 2)], y_rs.at[2 + way])
            pass_on(3)
            sib_wait(0, 1)
            sib_wait(0, 2)

        @pl.when(u == 3)
        def _():
            z_arrival(1)
            sib_wait(0, 3)

        mid = ((u + 1) // 2) % 2
        blocks = []
        for j in range(2):
            half = (core + (1 - mid) * j + mid * (u // 2)) % 2
            dy = mid * (1 + 2 * j) + (1 - mid) * 2 * (u // 3)
            blocks.append((half, z, (y + dy) % 4))
        accumulate(blocks)
        return carry

    lax.fori_loop(0, 4, near, 0)

    def beyond(s, carry):
        @pl.when(s == 0)
        def _():
            z_arrival(2)
            sib_wait(3, 0)
            sib_wait(1, 0)

        @pl.when(s == 1)
        def _():
            z_arrival(3)
            sib_wait(3, 1)
            sib_wait(1, 1)

        @pl.when(s == 2)
        def _():
            far_arrival(0)
            far_arrival(1)
            sib_wait(3, 2)
            sib_wait(1, 2)

        @pl.when(s == 3)
        def _():
            far_arrival(2)
            far_arrival(3)
            sib_wait(3, 3)
            sib_wait(1, 3)

        @pl.when(s == 4)
        def _():
            sib_wait(2, 0)
            sib_wait(2, 1)

        @pl.when(s == 5)
        def _():
            sib_wait(2, 2)
            sib_wait(2, 3)

        far = s // 4
        blocks = []
        for j in range(4):
            dz = (1 - far) * (3 - 2 * (j % 2)) + 2 * far
            i = (1 - far) * s + far * (2 * (s - 4) + j % 2)
            blocks.append(((core + j // 2) % 2, (z + dz) % 4, (y + order(i)) % 4))
        accumulate(blocks)
        return carry

    lax.fori_loop(0, 6, beyond, 0)

    for n in range(NODES):
        base = n * COLS
        gl = acc[base : base + CLASSES, :]
        hl = acc[base + CLASSES : base + COLS, :]
        whole_g = acc[base : base + CLASSES, BINS - 1 : BINS]
        whole_h = acc[base + CLASSES : base + COLS, BINS - 1 : BINS]
        gr = whole_g - gl
        hr = whole_h - hl
        score = (
            gl * gl / (hl + RIDGE)
            + gr * gr / (hr + RIDGE)
            - whole_g * whole_g / (whole_h + RIDGE)
        )
        gain = jnp.sum(score, axis=0, keepdims=True) * (1.0 / CLASSES)
        for k in range(4):
            gain_send[n // 2, (n % 2) * 4 + k : (n % 2) * 4 + k + 1, :] = gain[
                :, k * LANES : (k + 1) * LANES
            ]

    def out_copy(d):
        to = (row + d) % NR
        return send(
            gain_send.at[to], gain_recv.at[row], out_ss.at[d], out_rs.at[d], to, feat
        )

    for d in range(1, NR):
        out_copy(d).start()
    gain_ref[row] = gain_send[row]
    for d in range(1, NR):
        came = (row + NR - d) % NR
        at = gain_recv.at[came]
        send(at, at, out_ss.at[d], out_rs.at[d], row, feat).wait_recv()
        gain_ref[came] = gain_recv[came]

    totals = unit_tot[0]
    for u in range(1, 32):
        totals = totals + unit_tot[u]
    total_ref[...] = totals

    for d in range(1, NF):
        bit_copy(d).wait_send()
    for d in range(1, NR):
        bin_copy(d).wait_send()
        node_copy(d).wait_send()
        out_copy(d).wait_send()
    for d in range(1, 4):
        x_copy(d).wait_send()
    for way in range(2):
        y_copy(way).wait_send()
        y_far_copy(way).wait_send()
    for i in range(4):
        z_copy(0, i).wait_send()
        z_copy(1, i).wait_send()
        far_copy(i).wait_send()
        for dz in range(4):
            sib_copy(dz, i).wait_send()


def body(margins, labels, row_bins, parents, split_feature, split_bin, leaf_values):
    vmem = pl.BlockSpec(memory_space=pltpu.VMEM)
    hbm = pl.BlockSpec(memory_space=pltpu.HBM)
    dma = pltpu.SemaphoreType.DMA
    gains, totals = pl.pallas_call(
        kernel,
        out_shape=(
            jax.ShapeDtypeStruct((NR, 8, LANES), F32),
            jax.ShapeDtypeStruct((NODES, COLS), F32),
        ),
        in_specs=[hbm] * 8,
        out_specs=(vmem, vmem),
        scratch_shapes=[
            pltpu.SMEM((PARENTS,), jnp.int32),
            pltpu.SMEM((PARENTS,), jnp.int32),
            pltpu.VMEM((CLASSES, OWN), F32),
            pltpu.VMEM((1, OWN), jnp.int32),
            pltpu.VMEM((FD, GROUP), jnp.int32),
            pltpu.VMEM((KB, LANES), jnp.int32),
            pltpu.VMEM((1, GROUP), jnp.int32),
            pltpu.VMEM((NODES, CLASSES), F32),
            pltpu.VMEM((32, LANES), F32),
            pltpu.VMEM((32, LANES), BF),
            pltpu.VMEM((NF, 32, LANES), BF),
            pltpu.VMEM((NR, KB * FL, LANES), BF),
            pltpu.VMEM((NR, KB * FL, LANES), BF),
            pltpu.VMEM((NR, KB, FL, LANES), F32),
            pltpu.VMEM((NR, KB, LANES), F32),
            pltpu.VMEM((4, 2, 96, LANES), BF),
            pltpu.VMEM((2, 4, 4, 4, 96, LANES), BF),
            pltpu.VMEM((NODES * COLS, FL * BINS), F32),
            pltpu.VMEM((32, NODES, COLS), F32),
            pltpu.VMEM((NR, 8, LANES), F32),
            pltpu.VMEM((NR, 8, LANES), F32),
            dma((8,)),
            dma((NF,)), dma((NF,)), dma((NR,)), dma((NR,)), dma((NR,)), dma((NR,)),
            dma((4,)), dma((4,)), dma((4,)), dma((4,)),
            dma((2, 4)), dma((2, 4)), dma((4,)), dma((4,)), dma((4, 4)), dma((4, 4)),
            dma((NR,)), dma((NR,)),
        ],
        compiler_params=pltpu.CompilerParams(
            collective_id=0, has_side_effects=True, vmem_limit_bytes=58 << 20
        ),
    )(
        split_feature,
        split_bin,
        margins.T,
        labels.reshape(1, OWN),
        row_bins,
        parents.reshape(KB, LANES),
        parents.reshape(1, GROUP),
        leaf_values,
    )
    shaped = gains.reshape(NR, 2, 4, 2, BINS).transpose(1, 0, 2, 3, 4)
    return shaped.reshape(2, FD, BINS), totals


def solution(mesh):
    return jax.shard_map(
        body,
        mesh=mesh,
        in_specs=(
            P(("rows", "feat"), None),
            P(("rows", "feat")),
            P("feat", "rows"),
            P("rows"),
            P(),
            P(),
            P(),
        ),
        out_specs=(P("rows", "feat", None), P()),
        check_vma=False,
    )
```

```python
import jax
import jax.numpy as jnp
from jax import lax
from jax.experimental import pallas as pl
from jax.experimental.pallas import tpu as pltpu
from jax.sharding import PartitionSpec as P

MESH = pl.DeviceIdType.MESH
BINS = 64
NODES = 16
CLASSES = 32
COLS = 2 * CLASSES
PARENTS = 8
RIDGE = 1.0
LANES = 128
NR = 8
NF = 16
OWN = 192
GROUP = 3072
KB = GROUP // LANES
FD = 64
FL = FD // NR
FAR_FIRST = (10, 6, 14, 9, 11, 8, 2, 5, 7, 13, 15, 4, 12, 1, 3)
ROW_ORDER = ((0, 1), (1, 0), (1, 1), (3, 0), (3, 1), (2, 0), (2, 1))
FAR_ROWS = (5, 6, 1, 2, 3, 4, 0)
BF = jnp.bfloat16
F32 = jnp.float32


def own_gradients(margins, labels, parents, leaf_t, side):
    leaf = jnp.zeros(margins.shape, F32)
    for p in range(PARENTS):
        column = leaf_t[:, 2 * p + side : 2 * p + side + 1]
        leaf = jnp.where(parents == p, column, leaf)
    logits = margins + leaf
    top = jnp.max(logits, axis=0, keepdims=True)
    grown = jnp.exp(logits - top)
    prob = grown / jnp.sum(grown, axis=0, keepdims=True)
    classes = lax.broadcasted_iota(jnp.int32, margins.shape, 0)
    hot = jnp.where(classes == labels, 1.0, 0.0)
    return prob - hot, 2.0 * prob * (1.0 - prob)


def kernel(
    sf_hbm, sb_hbm, margin_hbm, label_hbm, bins_hbm, par_hbm, parrow_hbm, leaf_hbm,
    gain_ref, total_ref,
    sf_ref, sb_ref, margin_ref, label_ref, bins_ref, par_ref, parrow_ref, leaf_ref,
    bit_f32, bit_send, bit_recv, bin_send, bin_recv, bin_all, node_all,
    spec, grads, acc, unit_tot, gain_send, gain_recv,
    in_sem, bit_ss, bit_rs, bin_ss, bin_rs, node_ss, node_rs, x_ss, x_rs,
    z_ss, z_rs, y_ss, y_rs, far_ss, far_rs, sib_ss, sib_rs, out_ss, out_rs,
):
    row = lax.axis_index("rows")
    feat = lax.axis_index("feat")
    y, core = row // 2, row % 2
    z, x = feat // 4, feat % 4
    odd = feat % 2

    def send(src, dst, ss, rs, r, f):
        return pltpu.make_async_remote_copy(
            src_ref=src, dst_ref=dst, send_sem=ss, recv_sem=rs,
            device_id=(r, f), device_id_type=MESH,
        )

    barrier = pltpu.get_barrier_semaphore()
    for d in FAR_FIRST:
        pl.semaphore_signal(barrier, inc=1, device_id=(row, (feat + d) % NF), device_id_type=MESH)
    for d in range(1, NR):
        pl.semaphore_signal(barrier, inc=1, device_id=((row + d) % NR, feat), device_id_type=MESH)

    inputs = [
        pltpu.make_async_copy(src, dst, in_sem.at[k])
        for k, (src, dst) in enumerate((
            (bins_hbm, bins_ref), (parrow_hbm, parrow_ref), (sf_hbm, sf_ref),
            (sb_hbm, sb_ref), (margin_hbm, margin_ref), (label_hbm, label_ref),
            (par_hbm, par_ref), (leaf_hbm, leaf_ref),
        ))
    ]
    for copy in inputs:
        copy.start()
    for copy in inputs:
        copy.wait()

    right = jnp.zeros((1, GROUP), F32)
    for p in range(PARENTS):
        local = sf_ref[p] - feat * FD
        owned = jnp.logical_and(local >= 0, local < FD).astype(jnp.int32)
        at = jnp.minimum(jnp.maximum(local, 0), FD - 1)
        limit = sb_ref[p] * owned + BINS * (1 - owned)
        hit = jnp.logical_and(bins_ref[pl.ds(at, 1), :] > limit, parrow_ref[...] == p)
        right = jnp.where(hit, 1.0, right)
    bit_f32[...] = jnp.zeros_like(bit_f32)
    for k in range(KB):
        bit_f32[k : k + 1, :] = right[:, k * LANES : (k + 1) * LANES]
    bit_send[...] = bit_f32[...].astype(BF)

    def arrange(value):
        padded = jnp.concatenate(
            [value, jnp.zeros((value.shape[0], 2 * LANES - OWN), value.dtype)], axis=1
        )
        turned = jnp.concatenate([padded[:, 64:], padded[:, :64]], axis=1)
        return jnp.where(odd == 1, turned, padded)

    def rows_of(ref, pair, side):
        main = ref[pl.ds(3 * pair + 2 * side, 1), :]
        rest = ref[pl.ds(3 * pair + 1, 1), :]
        return main, rest

    margins = arrange(margin_ref[...])
    labels = arrange(label_ref[...])
    own_parents = jnp.concatenate(rows_of(par_ref, feat // 2, odd), axis=1)
    leaf_t = leaf_ref[...].T
    first_half = lax.broadcasted_iota(jnp.int32, (CLASSES, LANES), 1) < 64
    keep = first_half == (odd == 0)
    for side in range(2):
        g, h = own_gradients(margins, labels, own_parents, leaf_t, side)
        rest = jnp.where(keep, g[:, LANES:], pltpu.roll(h[:, LANES:], 64, 1))
        spec[x, side] = jnp.concatenate([g[:, :LANES], h[:, :LANES], rest], axis=0).astype(BF)

    def load_bins(to):
        first = pl.multiple_of(to * FL, FL)
        return [
            bins_ref[pl.ds(first, FL), k * LANES : (k + 1) * LANES].astype(F32)
            for k in range(KB)
        ]

    def row_at(dy, other):
        return 2 * ((y + dy) % 4) + (core + other) % 2

    for d, (dy, other) in enumerate(ROW_ORDER):
        bin_send[d] = jnp.concatenate(load_bins(row_at(dy, other)), axis=0).astype(BF)
    for k, part in enumerate(load_bins(row)):
        bin_all[row, k] = part

    def bit_copy(d):
        return send(
            bit_send, bit_recv.at[d], bit_ss.at[d], bit_rs.at[d], row, (feat + d) % NF
        )

    def x_copy(d):
        at = spec.at[x]
        return send(at, at, x_ss.at[d], x_rs.at[d], row, 4 * z + (x + d) % 4)

    def bin_copy(d):
        to = row_at(*ROW_ORDER[d])
        return send(bin_send.at[d], bin_recv.at[d], bin_ss.at[d], bin_rs.at[d], to, feat)

    def node_copy(d):
        to = row_at(*ROW_ORDER[d])
        return send(node_all.at[row], node_all.at[row], node_ss.at[d], node_rs.at[d], to, feat)

    def arrived(at, sem):
        send(at, at, sem, sem, row, feat).wait_recv()

    def order(i):
        return i + i // 2 - 2 * (i // 3)

    def block(half, dz, dy):
        return grads.at[half, (z + dz) % 4, (y + dy) % 4]

    def z_copy(way):
        at = block(core, 0, 0)
        to = 4 * ((z + 1 + 2 * way) % 4) + x
        return send(at, at, z_ss.at[way], z_rs.at[way], row, to)

    def z_far_copy(way):
        at = block(core, 3 - 2 * way, 0).at[pl.ds(2 * way, 2)]
        to = 4 * ((z + 1 + 2 * way) % 4) + x
        return send(at, at, z_ss.at[2 + way], z_rs.at[2 + way], row, to)

    def y_copy(way, i):
        at = block(core, order(i), 0)
        return send(at, at, y_ss.at[way, i], y_rs.at[way, i], row_at(1 + 2 * way, 0), feat)

    def y_far_copy(i):
        way = i // 2
        at = block(core, order(i), 3 - 2 * way)
        return send(at, at, far_ss.at[i], far_rs.at[i], row_at(1 + 2 * way, 0), feat)

    def sib_copy(dy, i):
        at = block(core, order(i), dy)
        return send(at, at, sib_ss.at[dy, i], sib_rs.at[dy, i], row_at(0, 1), feat)

    def sib_wait(dy, i):
        arrived(block(1 - core, order(i), dy), sib_rs.at[dy, i])

    def pass_on(i):
        sib_copy(0, i).start()
        y_copy(0, i).start()
        y_copy(1, i).start()

    def y_arrival(i):
        for way in range(2):
            arrived(block(core, order(i), 3 - 2 * way), y_rs.at[way, i])
            if i // 2 == way:
                y_far_copy(i).start()
            sib_copy(3 - 2 * way, i).start()

    def far_arrival(i):
        arrived(block(core, order(i), 2), far_rs.at[i])
        sib_copy(2, i).start()

    def row_arrival(d):
        bin_copy(d).wait_recv()
        dy, other = ROW_ORDER[d]
        came = row_at(4 - dy, other)
        part = bin_recv[d].astype(F32)
        for k in range(KB):
            bin_all[came, k] = part[k * FL : (k + 1) * FL]
        arrived(node_all.at[came], node_rs.at[d])

    pl.semaphore_wait(barrier, NF - 1 + NR - 1)
    for d in FAR_FIRST:
        bit_copy(d).start()
    for d in (1, 3, 2):
        x_copy(d).start()
    for d in range(NR - 1):
        bin_copy(d).start()

    acc[...] = jnp.zeros_like(acc)

    bits = bit_send[...].astype(F32)
    for d in range(1, NF):
        bit_copy(d).wait_recv()
        bits = bits + bit_recv[d].astype(F32)
    node_all[row] = (2 * par_ref[...]).astype(F32) + bits[:KB]
    bit_f32[...] = bits
    for d in range(NR - 1):
        node_copy(d).start()

    for d in (1, 3, 2):
        arrived(spec.at[(x + 4 - d) % 4], x_rs.at[d])
    for xx in range(4):
        main, rest = rows_of(bit_f32, 2 * z + xx // 2, xx % 2)
        low = lax.broadcasted_iota(jnp.int32, (1, LANES), 1) < 64
        turned = jnp.concatenate([rest[:, 64:], rest[:, :64]], axis=1)
        rest = jnp.where(low, rest, turned) if xx % 2 == 0 else jnp.where(low, turned, rest)
        side = jnp.concatenate(
            [jnp.broadcast_to(main, (64, LANES)), jnp.broadcast_to(rest, (32, LANES))], axis=0
        ).astype(BF)
        grads[core, z, y, xx] = jnp.where(side > BF(0.5), spec[xx, 1], spec[xx, 0])
    sib_copy(0, 0).start()
    z_copy(0).start()
    z_copy(1).start()
    y_copy(0, 0).start()
    y_copy(1, 0).start()
    row_arrival(0)

    lane_low = lax.broadcasted_iota(jnp.int32, (32, LANES), 1) < 64
    bin_ids = lax.broadcasted_iota(jnp.int32, (BINS, LANES), 0).astype(F32).astype(BF)
    node_ids = lax.broadcasted_iota(jnp.int32, (NODES, LANES), 0).astype(F32).astype(BF)
    contract = (((1,), (1,)), ((), ()))

    def accumulate(blocks):
        weighted, masks = [], []
        for half, zz, yy in blocks:
            group = 2 * yy + half
            hots, pieces = [], []
            for q in range(2):
                even = grads[half, zz, yy, 2 * q]
                last = grads[half, zz, yy, 2 * q + 1]
                rest_e, rest_o = even[64:], last[64:]
                low = jnp.where(lane_low, rest_e, rest_o)
                high = jnp.where(lane_low, rest_o, rest_e).astype(F32)
                high = pltpu.roll(high, 64, 1).astype(BF)
                middle = jnp.concatenate([low, high], axis=0)
                first = 3 * (2 * zz + q)
                for i, piece in enumerate((even[:64], middle, last[:64])):
                    nodes = node_all[group, pl.ds(first + i, 1), :].astype(BF)
                    wide = jnp.broadcast_to(nodes, (COLS, LANES))
                    zero = jnp.zeros_like(piece)
                    weighted.append(
                        jnp.concatenate(
                            [jnp.where(wide == BF(n), piece, zero) for n in range(NODES)],
                            axis=0,
                        )
                    )
                    same = jnp.broadcast_to(nodes, (NODES, LANES)) == node_ids
                    hots.append(jnp.where(same, BF(1), BF(0)))
                    pieces.append(piece)
                    rows = []
                    for f in range(FL):
                        here = bin_all[group, first + i, f : f + 1, :].astype(BF)
                        under = jnp.broadcast_to(here, (BINS, LANES)) <= bin_ids
                        rows.append(jnp.where(under, BF(1), BF(0)))
                    masks.append(jnp.concatenate(rows, axis=0))
            unit_tot[(half * 4 + zz) * 4 + yy] = lax.dot_general(
                jnp.concatenate(hots, axis=1),
                jnp.concatenate(pieces, axis=1),
                contract,
                preferred_element_type=F32,
            )
        acc[...] += lax.dot_general(
            jnp.concatenate(weighted, axis=1),
            jnp.concatenate(masks, axis=1),
            contract,
            preferred_element_type=F32,
        )

    def first(u, carry):
        @pl.when(u == 1)
        def _():
            sib_wait(0, 0)

        accumulate([((core + u) % 2, z, y)])
        return carry

    lax.fori_loop(0, 2, first, 0)

    def near(u, carry):
        @pl.when(u == 0)
        def _():
            for way in range(2):
                arrived(block(core, 3 - 2 * way, 0), z_rs.at[way])
                z_far_copy(way).start()
            pass_on(1)
            pass_on(2)

        @pl.when(u == 1)
        def _():
            sib_wait(0, 1)
            sib_wait(0, 2)

        @pl.when(u == 2)
        def _():
            for way in range(2):
                arrived(block(core, 2, 0).at[pl.ds(2 * way, 2)], z_rs.at[2 + way])
            pass_on(3)
            y_arrival(0)
            sib_wait(0, 3)

        last = u // 2
        blocks = []
        for j in range(2):
            half = (core + (1 - last) * u + last * j) % 2
            dz = (1 - last) * (1 + 2 * j) + 2 * last
            blocks.append((half, (z + dz) % 4, y))
        accumulate(blocks)
        return carry

    lax.fori_loop(0, 3, near, 0)

    for d in range(1, NR - 1):
        row_arrival(d)

    def beyond(s, carry):
        @pl.when(s == 0)
        def _():
            y_arrival(1)
            sib_wait(3, 0)
            sib_wait(1, 0)

        @pl.when(s == 1)
        def _():
            y_arrival(2)
            sib_wait(3, 1)
            sib_wait(1, 1)

        @pl.when(s == 2)
        def _():
            y_arrival(3)
            far_arrival(0)
            far_arrival(1)
            sib_wait(3, 2)
            sib_wait(1, 2)

        @pl.when(s == 3)
        def _():
            far_arrival(2)
            far_arrival(3)
            sib_wait(3, 3)
            sib_wait(1, 3)

        @pl.when(s == 4)
        def _():
            sib_wait(2, 0)
            sib_wait(2, 1)

        @pl.when(s == 5)
        def _():
            sib_wait(2, 2)
            sib_wait(2, 3)

        far = s // 4
        blocks = []
        for j in range(4):
            dy = (1 - far) * (3 - 2 * (j % 2)) + 2 * far
            i = (1 - far) * s + far * (2 * (s - 4) + j % 2)
            blocks.append(((core + j // 2) % 2, (z + order(i)) % 4, (y + dy) % 4))
        accumulate(blocks)
        return carry

    lax.fori_loop(0, 6, beyond, 0)

    for n in range(NODES):
        base = n * COLS
        gl = acc[base : base + CLASSES, :]
        hl = acc[base + CLASSES : base + COLS, :]
        whole_g = acc[base : base + CLASSES, BINS - 1 : BINS]
        whole_h = acc[base + CLASSES : base + COLS, BINS - 1 : BINS]
        gr = whole_g - gl
        hr = whole_h - hl
        score = (
            gl * gl / (hl + RIDGE)
            + gr * gr / (hr + RIDGE)
            - whole_g * whole_g / (whole_h + RIDGE)
        )
        gain = jnp.sum(score, axis=0, keepdims=True) * (1.0 / CLASSES)
        for f in range(FL):
            gain_send[n // 2, n % 2, f : f + 1, :] = gain[:, f * BINS : (f + 1) * BINS]

    def gain_at(r):
        return gain_recv.at[:, pl.ds(pl.multiple_of(r * FL, FL), FL)]

    def out_copy(d):
        to = row_at(*ROW_ORDER[d])
        return send(gain_send.at[to], gain_at(row), out_ss.at[d], out_rs.at[d], to, feat)

    for d in FAR_ROWS:
        out_copy(d).start()
    for n in range(2):
        gain_recv[n, pl.ds(pl.multiple_of(row * FL, FL), FL)] = gain_send[row, n]
    totals = unit_tot[0]
    for u in range(1, 32):
        totals = totals + unit_tot[u]
    total_ref[...] = totals
    for d in range(NR - 1):
        dy, other = ROW_ORDER[d]
        arrived(gain_at(row_at(4 - dy, other)), out_rs.at[d])
    gain_ref[...] = gain_recv[...]

    for d in range(1, NF):
        bit_copy(d).wait_send()
    for d in range(NR - 1):
        bin_copy(d).wait_send()
        node_copy(d).wait_send()
        out_copy(d).wait_send()
    for d in range(1, 4):
        x_copy(d).wait_send()
    for way in range(2):
        z_copy(way).wait_send()
        z_far_copy(way).wait_send()
    for i in range(4):
        y_copy(0, i).wait_send()
        y_copy(1, i).wait_send()
        y_far_copy(i).wait_send()
        for dy in range(4):
            sib_copy(dy, i).wait_send()


def body(margins, labels, row_bins, parents, split_feature, split_bin, leaf_values):
    vmem = pl.BlockSpec(memory_space=pltpu.VMEM)
    hbm = pl.BlockSpec(memory_space=pltpu.HBM)
    dma = pltpu.SemaphoreType.DMA
    return pl.pallas_call(
        kernel,
        out_shape=(
            jax.ShapeDtypeStruct((2, FD, BINS), F32),
            jax.ShapeDtypeStruct((NODES, COLS), F32),
        ),
        in_specs=[hbm] * 8,
        out_specs=(vmem, vmem),
        scratch_shapes=[
            pltpu.SMEM((PARENTS,), jnp.int32),
            pltpu.SMEM((PARENTS,), jnp.int32),
            pltpu.VMEM((CLASSES, OWN), F32),
            pltpu.VMEM((1, OWN), jnp.int32),
            pltpu.VMEM((FD, GROUP), jnp.int32),
            pltpu.VMEM((KB, LANES), jnp.int32),
            pltpu.VMEM((1, GROUP), jnp.int32),
            pltpu.VMEM((NODES, CLASSES), F32),
            pltpu.VMEM((32, LANES), F32),
            pltpu.VMEM((32, LANES), BF),
            pltpu.VMEM((NF, 32, LANES), BF),
            pltpu.VMEM((NR, KB * FL, LANES), BF),
            pltpu.VMEM((NR, KB * FL, LANES), BF),
            pltpu.VMEM((NR, KB, FL, LANES), F32),
            pltpu.VMEM((NR, KB, LANES), F32),
            pltpu.VMEM((4, 2, 96, LANES), BF),
            pltpu.VMEM((2, 4, 4, 4, 96, LANES), BF),
            pltpu.VMEM((NODES * COLS, FL * BINS), F32),
            pltpu.VMEM((32, NODES, COLS), F32),
            pltpu.VMEM((NR, 2, FL, BINS), F32),
            pltpu.VMEM((2, FD, BINS), F32),
            dma((8,)),
            dma((NF,)), dma((NF,)), dma((NR,)), dma((NR,)), dma((NR,)), dma((NR,)),
            dma((4,)), dma((4,)), dma((4,)), dma((4,)),
            dma((2, 4)), dma((2, 4)), dma((4,)), dma((4,)), dma((4, 4)), dma((4, 4)),
            dma((NR,)), dma((NR,)),
        ],
        compiler_params=pltpu.CompilerParams(
            collective_id=0, has_side_effects=True, vmem_limit_bytes=58 << 20
        ),
    )(
        split_feature,
        split_bin,
        margins.T,
        labels.reshape(1, OWN),
        row_bins,
        parents.reshape(KB, LANES),
        parents.reshape(1, GROUP),
        leaf_values,
    )


def solution(mesh):
    return jax.shard_map(
        body,
        mesh=mesh,
        in_specs=(
            P(("rows", "feat"), None),
            P(("rows", "feat")),
            P("feat", "rows"),
            P("rows"),
            P(),
            P(),
            P(),
        ),
        out_specs=(P("rows", "feat", None), P()),
        check_vma=False,
    )
```

```python
import jax
import jax.numpy as jnp
from jax import lax
from jax.experimental import pallas as pl
from jax.experimental.pallas import tpu as pltpu
from jax.sharding import PartitionSpec as P

MESH = pl.DeviceIdType.MESH
BINS = 64
NODES = 16
CLASSES = 32
COLS = 2 * CLASSES
PARENTS = 8
RIDGE = 1.0
LANES = 128
NR = 8
NF = 16
OWN = 192
GROUP = 3072
KB = GROUP // LANES
FD = 64
FL = FD // NR
FAR_FIRST = (10, 6, 14, 9, 11, 8, 2, 5, 7, 13, 15, 4, 12, 1, 3)
ROW_ORDER = ((0, 1), (1, 0), (1, 1), (3, 0), (3, 1), (2, 0), (2, 1))
FAR_ROWS = (5, 6, 1, 2, 3, 4, 0)
BF = jnp.bfloat16
F32 = jnp.float32


def own_gradients(margins, labels, parents, leaf_t, side):
    leaf = jnp.zeros(margins.shape, F32)
    for p in range(PARENTS):
        column = leaf_t[:, 2 * p + side : 2 * p + side + 1]
        leaf = jnp.where(parents == p, column, leaf)
    logits = margins + leaf
    top = jnp.max(logits, axis=0, keepdims=True)
    grown = jnp.exp(logits - top)
    prob = grown / jnp.sum(grown, axis=0, keepdims=True)
    classes = lax.broadcasted_iota(jnp.int32, margins.shape, 0)
    hot = jnp.where(classes == labels, 1.0, 0.0)
    return prob - hot, 2.0 * prob * (1.0 - prob)


def kernel(
    sf_hbm, sb_hbm, margin_hbm, label_hbm, bins_hbm, par_hbm, parrow_hbm, leaf_hbm,
    gain_ref, total_ref,
    sf_ref, sb_ref, margin_ref, label_ref, bins_ref, par_ref, parrow_ref, leaf_ref,
    bit_f32, bit_send, bit_recv, bin_send, bin_recv, bin_all, node_all,
    spec, grads, acc, chunk_tot, group_tot, gain_send, gain_recv,
    in_sem, bit_ss, bit_rs, bin_ss, bin_rs, node_ss, node_rs, x_ss, x_rs,
    z_ss, z_rs, y_ss, y_rs, far_ss, far_rs, sib_ss, sib_rs, out_ss, out_rs,
    ct_ss, ct_rs, gt_ss, gt_rs,
):
    row = lax.axis_index("rows")
    feat = lax.axis_index("feat")
    y, core = row // 2, row % 2
    z, x = feat // 4, feat % 4
    odd = feat % 2

    def send(src, dst, ss, rs, r, f):
        return pltpu.make_async_remote_copy(
            src_ref=src, dst_ref=dst, send_sem=ss, recv_sem=rs,
            device_id=(r, f), device_id_type=MESH,
        )

    barrier = pltpu.get_barrier_semaphore()
    for d in FAR_FIRST:
        pl.semaphore_signal(barrier, inc=1, device_id=(row, (feat + d) % NF), device_id_type=MESH)
    for d in range(1, NR):
        pl.semaphore_signal(barrier, inc=1, device_id=((row + d) % NR, feat), device_id_type=MESH)

    inputs = [
        pltpu.make_async_copy(src, dst, in_sem.at[k])
        for k, (src, dst) in enumerate((
            (bins_hbm, bins_ref), (parrow_hbm, parrow_ref), (sf_hbm, sf_ref),
            (sb_hbm, sb_ref), (margin_hbm, margin_ref), (label_hbm, label_ref),
            (par_hbm, par_ref), (leaf_hbm, leaf_ref),
        ))
    ]
    for copy in inputs:
        copy.start()
    for copy in inputs:
        copy.wait()

    right = jnp.zeros((1, GROUP), F32)
    for p in range(PARENTS):
        local = sf_ref[p] - feat * FD
        owned = jnp.logical_and(local >= 0, local < FD).astype(jnp.int32)
        at = jnp.minimum(jnp.maximum(local, 0), FD - 1)
        limit = sb_ref[p] * owned + BINS * (1 - owned)
        hit = jnp.logical_and(bins_ref[pl.ds(at, 1), :] > limit, parrow_ref[...] == p)
        right = jnp.where(hit, 1.0, right)
    bit_f32[...] = jnp.zeros_like(bit_f32)
    for k in range(KB):
        bit_f32[k : k + 1, :] = right[:, k * LANES : (k + 1) * LANES]
    bit_send[...] = bit_f32[...].astype(BF)

    def arrange(value):
        padded = jnp.concatenate(
            [value, jnp.zeros((value.shape[0], 2 * LANES - OWN), value.dtype)], axis=1
        )
        turned = jnp.concatenate([padded[:, 64:], padded[:, :64]], axis=1)
        return jnp.where(odd == 1, turned, padded)

    def rows_of(ref, pair, side):
        main = ref[pl.ds(3 * pair + 2 * side, 1), :]
        rest = ref[pl.ds(3 * pair + 1, 1), :]
        return main, rest

    margins = arrange(margin_ref[...])
    labels = arrange(label_ref[...])
    own_parents = jnp.concatenate(rows_of(par_ref, feat // 2, odd), axis=1)
    leaf_t = leaf_ref[...].T
    first_half = lax.broadcasted_iota(jnp.int32, (CLASSES, LANES), 1) < 64
    keep = first_half == (odd == 0)
    for side in range(2):
        g, h = own_gradients(margins, labels, own_parents, leaf_t, side)
        rest = jnp.where(keep, g[:, LANES:], pltpu.roll(h[:, LANES:], 64, 1))
        spec[x, side] = jnp.concatenate([g[:, :LANES], h[:, :LANES], rest], axis=0).astype(BF)

    def load_bins(to):
        first = pl.multiple_of(to * FL, FL)
        return [
            bins_ref[pl.ds(first, FL), k * LANES : (k + 1) * LANES].astype(F32)
            for k in range(KB)
        ]

    def row_at(dy, other):
        return 2 * ((y + dy) % 4) + (core + other) % 2

    def bit_copy(d):
        return send(
            bit_send, bit_recv.at[d], bit_ss.at[d], bit_rs.at[d], row, (feat + d) % NF
        )

    def x_copy(d):
        at = spec.at[x]
        return send(at, at, x_ss.at[d], x_rs.at[d], row, 4 * z + (x + d) % 4)

    def bin_copy(d):
        to = row_at(*ROW_ORDER[d])
        return send(bin_send.at[d], bin_recv.at[d], bin_ss.at[d], bin_rs.at[d], to, feat)

    def node_copy(d):
        to = row_at(*ROW_ORDER[d])
        return send(node_all.at[row], node_all.at[row], node_ss.at[d], node_rs.at[d], to, feat)

    def arrived(at, sem):
        send(at, at, sem, sem, row, feat).wait_recv()

    def order(i):
        return i + i // 2 - 2 * (i // 3)

    def block(half, dz, dy):
        return grads.at[half, (z + dz) % 4, (y + dy) % 4]

    def z_copy(way):
        at = block(core, 0, 0)
        to = 4 * ((z + 1 + 2 * way) % 4) + x
        return send(at, at, z_ss.at[way], z_rs.at[way], row, to)

    def z_far_copy(way):
        at = block(core, 3 - 2 * way, 0).at[pl.ds(2 * way, 2)]
        to = 4 * ((z + 1 + 2 * way) % 4) + x
        return send(at, at, z_ss.at[2 + way], z_rs.at[2 + way], row, to)

    def y_copy(way, i):
        at = block(core, order(i), 0)
        return send(at, at, y_ss.at[way, i], y_rs.at[way, i], row_at(1 + 2 * way, 0), feat)

    def y_far_copy(i):
        way = i // 2
        at = block(core, order(i), 3 - 2 * way)
        return send(at, at, far_ss.at[i], far_rs.at[i], row_at(1 + 2 * way, 0), feat)

    def sib_copy(dy, i):
        at = block(core, order(i), dy)
        return send(at, at, sib_ss.at[dy, i], sib_rs.at[dy, i], row_at(0, 1), feat)

    def sib_wait(dy, i):
        arrived(block(1 - core, order(i), dy), sib_rs.at[dy, i])

    def pass_on(i):
        sib_copy(0, i).start()
        y_copy(0, i).start()
        y_copy(1, i).start()

    def y_arrival(i):
        for way in range(2):
            arrived(block(core, order(i), 3 - 2 * way), y_rs.at[way, i])
            if i // 2 == way:
                y_far_copy(i).start()
            sib_copy(3 - 2 * way, i).start()

    def far_arrival(i):
        arrived(block(core, order(i), 2), far_rs.at[i])
        sib_copy(2, i).start()

    def row_arrival(d):
        bin_copy(d).wait_recv()
        dy, other = ROW_ORDER[d]
        came = row_at(4 - dy, other)
        part = bin_recv[d].astype(F32)
        for k in range(KB):
            bin_all[came, k] = part[k * FL : (k + 1) * FL]
        arrived(node_all.at[came], node_rs.at[d])

    pl.semaphore_wait(barrier, NF - 1 + NR - 1)
    for d in FAR_FIRST:
        bit_copy(d).start()
    for d in (1, 3, 2):
        x_copy(d).start()
    for d, (dy, other) in enumerate(ROW_ORDER):
        bin_send[d] = jnp.concatenate(load_bins(row_at(dy, other)), axis=0).astype(BF)
        bin_copy(d).start()
    for k, part in enumerate(load_bins(row)):
        bin_all[row, k] = part

    acc[...] = jnp.zeros_like(acc)

    bits = bit_send[...].astype(F32)
    for d in range(1, NF):
        bit_copy(d).wait_recv()
        bits = bits + bit_recv[d].astype(F32)
    node_all[row] = (2 * par_ref[...]).astype(F32) + bits[:KB]
    bit_f32[...] = bits
    for d in range(NR - 1):
        node_copy(d).start()

    for d in (1, 3, 2):
        arrived(spec.at[(x + 4 - d) % 4], x_rs.at[d])
    for xx in range(4):
        main, rest = rows_of(bit_f32, 2 * z + xx // 2, xx % 2)
        low = lax.broadcasted_iota(jnp.int32, (1, LANES), 1) < 64
        turned = jnp.concatenate([rest[:, 64:], rest[:, :64]], axis=1)
        rest = jnp.where(low, rest, turned) if xx % 2 == 0 else jnp.where(low, turned, rest)
        side = jnp.concatenate(
            [jnp.broadcast_to(main, (64, LANES)), jnp.broadcast_to(rest, (32, LANES))], axis=0
        ).astype(BF)
        grads[core, z, y, xx] = jnp.where(side > BF(0.5), spec[xx, 1], spec[xx, 0])
    sib_copy(0, 0).start()
    z_copy(0).start()
    z_copy(1).start()
    y_copy(0, 0).start()
    y_copy(1, 0).start()
    row_arrival(0)

    lane_low = lax.broadcasted_iota(jnp.int32, (32, LANES), 1) < 64
    bin_ids = lax.broadcasted_iota(jnp.int32, (BINS, LANES), 0).astype(F32).astype(BF)
    node_ids = lax.broadcasted_iota(jnp.int32, (NODES, LANES), 0).astype(F32).astype(BF)
    contract = (((1,), (1,)), ((), ()))

    def pair_pieces(half, zz, yy, q):
        even = grads[half, zz, yy, 2 * q]
        last = grads[half, zz, yy, 2 * q + 1]
        rest_e, rest_o = even[64:], last[64:]
        low = jnp.where(lane_low, rest_e, rest_o)
        high = jnp.where(lane_low, rest_o, rest_e).astype(F32)
        high = pltpu.roll(high, 64, 1).astype(BF)
        return even[:64], jnp.concatenate([low, high], axis=0), last[:64]

    def accumulate(blocks):
        weighted, masks = [], []
        for half, zz, yy in blocks:
            group = 2 * yy + half
            for q in range(2):
                first = 3 * (2 * zz + q)
                for i, piece in enumerate(pair_pieces(half, zz, yy, q)):
                    nodes = node_all[group, pl.ds(first + i, 1), :].astype(BF)
                    wide = jnp.broadcast_to(nodes, (COLS, LANES))
                    zero = jnp.zeros_like(piece)
                    weighted.append(
                        jnp.concatenate(
                            [jnp.where(wide == BF(n), piece, zero) for n in range(NODES)],
                            axis=0,
                        )
                    )
                    rows = []
                    for f in range(FL):
                        here = bin_all[group, first + i, f : f + 1, :].astype(BF)
                        under = jnp.broadcast_to(here, (BINS, LANES)) <= bin_ids
                        rows.append(jnp.where(under, BF(1), BF(0)))
                    masks.append(jnp.concatenate(rows, axis=0))
        acc[...] += lax.dot_general(
            jnp.concatenate(weighted, axis=1),
            jnp.concatenate(masks, axis=1),
            contract,
            preferred_element_type=F32,
        )

    hots, pieces = [], []
    for q in range(2):
        for i, piece in enumerate(pair_pieces(core, z, y, q)):
            nodes = node_all[row, pl.ds(3 * (2 * z + q) + i, 1), :].astype(BF)
            same = jnp.broadcast_to(nodes, (NODES, LANES)) == node_ids
            hots.append(jnp.where(same, BF(1), BF(0)))
            pieces.append(piece)
    chunk_tot[z] = lax.dot_general(
        jnp.concatenate(hots, axis=1),
        jnp.concatenate(pieces, axis=1),
        contract,
        preferred_element_type=F32,
    )

    def chunk_tot_copy(d):
        at = chunk_tot.at[z]
        return send(at, at, ct_ss.at[d], ct_rs.at[d], row, 4 * ((z + d) % 4) + x)

    def group_tot_copy(d):
        at = group_tot.at[row]
        return send(at, at, gt_ss.at[d], gt_rs.at[d], row_at(*ROW_ORDER[d]), feat)

    for d in range(1, 4):
        chunk_tot_copy(d).start()

    def first(u, carry):
        @pl.when(u == 1)
        def _():
            sib_wait(0, 0)

        accumulate([((core + u) % 2, z, y)])
        return carry

    lax.fori_loop(0, 2, first, 0)

    def near(u, carry):
        @pl.when(u == 0)
        def _():
            for way in range(2):
                arrived(block(core, 3 - 2 * way, 0), z_rs.at[way])
                z_far_copy(way).start()
            pass_on(1)
            pass_on(2)

        @pl.when(u == 1)
        def _():
            sib_wait(0, 1)
            sib_wait(0, 2)

        half = (core + u) % 2
        accumulate([(half, (z + 1) % 4, y), (half, (z + 3) % 4, y)])
        return carry

    lax.fori_loop(0, 2, near, 0)

    for way in range(2):
        arrived(block(core, 2, 0).at[pl.ds(2 * way, 2)], z_rs.at[2 + way])
    pass_on(3)
    y_arrival(0)

    for d in range(1, NR - 1):
        row_arrival(d)

    for d in range(1, 4):
        arrived(chunk_tot.at[(z + 4 - d) % 4], ct_rs.at[d])
    group_tot[row] = (chunk_tot[0] + chunk_tot[1]) + (chunk_tot[2] + chunk_tot[3])
    for d in range(NR - 1):
        group_tot_copy(d).start()

    def beyond(s, carry):
        @pl.when(s == 0)
        def _():
            y_arrival(1)
            sib_wait(3, 0)
            sib_wait(1, 0)

        @pl.when(s == 1)
        def _():
            y_arrival(2)
            sib_wait(3, 1)
            sib_wait(1, 1)

        @pl.when(s == 2)
        def _():
            y_arrival(3)
            far_arrival(0)
            far_arrival(1)
            sib_wait(3, 2)
            sib_wait(1, 2)

        @pl.when(s == 3)
        def _():
            far_arrival(2)
            far_arrival(3)
            sib_wait(3, 3)
            sib_wait(1, 3)

        @pl.when(s == 4)
        def _():
            sib_wait(2, 0)
            sib_wait(2, 1)

        @pl.when(s == 5)
        def _():
            sib_wait(2, 2)
            sib_wait(2, 3)

        far = s // 4
        blocks = []
        for j in range(4):
            dy = (1 - far) * (3 - 2 * (j % 2)) + 2 * far
            i = (1 - far) * s + far * (2 * (s - 4) + j % 2)
            blocks.append(((core + j // 2) % 2, (z + order(i)) % 4, (y + dy) % 4))
        accumulate(blocks)
        return carry

    lax.fori_loop(0, 6, beyond, 0)

    sib_wait(0, 3)
    accumulate([(core, (z + 2) % 4, y), (1 - core, (z + 2) % 4, y)])

    for n in range(NODES):
        base = n * COLS
        gl = acc[base : base + CLASSES, :]
        hl = acc[base + CLASSES : base + COLS, :]
        whole_g = acc[base : base + CLASSES, BINS - 1 : BINS]
        whole_h = acc[base + CLASSES : base + COLS, BINS - 1 : BINS]
        gr = whole_g - gl
        hr = whole_h - hl
        score = (
            gl * gl / (hl + RIDGE)
            + gr * gr / (hr + RIDGE)
            - whole_g * whole_g / (whole_h + RIDGE)
        )
        gain = jnp.sum(score, axis=0, keepdims=True) * (1.0 / CLASSES)
        for k in range(4):
            at = (n % 2) * 4 + k
            gain_send[n // 2, at : at + 1, :] = gain[:, k * LANES : (k + 1) * LANES]

    def out_copy(d):
        to = row_at(*ROW_ORDER[d])
        return send(gain_send.at[to], gain_recv.at[row], out_ss.at[d], out_rs.at[d], to, feat)

    for d in FAR_ROWS:
        out_copy(d).start()
    gain_recv[row] = gain_send[row]
    for d in range(NR - 1):
        dy, other = ROW_ORDER[d]
        arrived(group_tot.at[row_at(4 - dy, other)], gt_rs.at[d])
    totals = group_tot[0]
    for r in range(1, NR):
        totals = totals + group_tot[r]
    total_ref[...] = totals

    for d in range(NR - 1):
        dy, other = ROW_ORDER[d]
        arrived(gain_recv.at[row_at(4 - dy, other)], out_rs.at[d])
    for r in range(NR):
        for n in range(2):
            tile = gain_recv[r, 4 * n : 4 * n + 4, :]
            for side in range(2):
                at = pl.ds(r * FL + side, 4, stride=2)
                gain_ref[n, at, :] = tile[:, side * BINS : (side + 1) * BINS]

    for d in range(1, NF):
        bit_copy(d).wait_send()
    for d in range(NR - 1):
        bin_copy(d).wait_send()
        node_copy(d).wait_send()
        out_copy(d).wait_send()
        group_tot_copy(d).wait_send()
    for d in range(1, 4):
        x_copy(d).wait_send()
        chunk_tot_copy(d).wait_send()
    for way in range(2):
        z_copy(way).wait_send()
        z_far_copy(way).wait_send()
    for i in range(4):
        y_copy(0, i).wait_send()
        y_copy(1, i).wait_send()
        y_far_copy(i).wait_send()
        for dy in range(4):
            sib_copy(dy, i).wait_send()


def body(margins, labels, row_bins, parents, split_feature, split_bin, leaf_values):
    vmem = pl.BlockSpec(memory_space=pltpu.VMEM)
    hbm = pl.BlockSpec(memory_space=pltpu.HBM)
    dma = pltpu.SemaphoreType.DMA
    return pl.pallas_call(
        kernel,
        out_shape=(
            jax.ShapeDtypeStruct((2, FD, BINS), F32),
            jax.ShapeDtypeStruct((NODES, COLS), F32),
        ),
        in_specs=[hbm] * 8,
        out_specs=(vmem, vmem),
        scratch_shapes=[
            pltpu.SMEM((PARENTS,), jnp.int32),
            pltpu.SMEM((PARENTS,), jnp.int32),
            pltpu.VMEM((CLASSES, OWN), F32),
            pltpu.VMEM((1, OWN), jnp.int32),
            pltpu.VMEM((FD, GROUP), jnp.int32),
            pltpu.VMEM((KB, LANES), jnp.int32),
            pltpu.VMEM((1, GROUP), jnp.int32),
            pltpu.VMEM((NODES, CLASSES), F32),
            pltpu.VMEM((32, LANES), F32),
            pltpu.VMEM((32, LANES), BF),
            pltpu.VMEM((NF, 32, LANES), BF),
            pltpu.VMEM((NR, KB * FL, LANES), BF),
            pltpu.VMEM((NR, KB * FL, LANES), BF),
            pltpu.VMEM((NR, KB, FL, LANES), F32),
            pltpu.VMEM((NR, KB, LANES), F32),
            pltpu.VMEM((4, 2, 96, LANES), BF),
            pltpu.VMEM((2, 4, 4, 4, 96, LANES), BF),
            pltpu.VMEM((NODES * COLS, FL * BINS), F32),
            pltpu.VMEM((4, NODES, COLS), F32),
            pltpu.VMEM((NR, NODES, COLS), F32),
            pltpu.VMEM((NR, 8, LANES), F32),
            pltpu.VMEM((NR, 8, LANES), F32),
            dma((8,)),
            dma((NF,)), dma((NF,)), dma((NR,)), dma((NR,)), dma((NR,)), dma((NR,)),
            dma((4,)), dma((4,)), dma((4,)), dma((4,)),
            dma((2, 4)), dma((2, 4)), dma((4,)), dma((4,)), dma((4, 4)), dma((4, 4)),
            dma((NR,)), dma((NR,)),
            dma((4,)), dma((4,)), dma((NR,)), dma((NR,)),
        ],
        compiler_params=pltpu.CompilerParams(
            collective_id=0, has_side_effects=True, vmem_limit_bytes=48 << 20
        ),
    )(
        *(
            pltpu.with_memory_space_constraint(value, pltpu.HBM)
            for value in (
                split_feature,
                split_bin,
                margins.T,
                labels.reshape(1, OWN),
                row_bins,
                parents.reshape(KB, LANES),
                parents.reshape(1, GROUP),
                leaf_values,
            )
        )
    )


def solution(mesh):
    return jax.shard_map(
        body,
        mesh=mesh,
        in_specs=(
            P(("rows", "feat"), None),
            P(("rows", "feat")),
            P("feat", "rows"),
            P("rows"),
            P(),
            P(),
            P(),
        ),
        out_specs=(P("rows", "feat", None), P()),
        check_vma=False,
    )
```

```python
import jax
import jax.numpy as jnp
from jax import lax
from jax.experimental import pallas as pl
from jax.experimental.pallas import tpu as pltpu
from jax.sharding import PartitionSpec as P

MESH = pl.DeviceIdType.MESH
BINS = 64
NODES = 16
CLASSES = 32
COLS = 2 * CLASSES
PARENTS = 8
RIDGE = 1.0
LANES = 128
NR = 8
NF = 16
OWN = 192
GROUP = 3072
KB = GROUP // LANES
FD = 64
FL = FD // NR
FAR_FIRST = (10, 6, 14, 9, 11, 8, 2, 5, 7, 13, 15, 4, 12, 1, 3)
ROW_ORDER = ((0, 1), (1, 0), (1, 1), (3, 0), (3, 1), (2, 0), (2, 1))
CHIP = 4
BF = jnp.bfloat16
F32 = jnp.float32


def own_gradients(margins, labels, parents, leaf_t, side):
    leaf = jnp.zeros(margins.shape, F32)
    for p in range(PARENTS):
        column = leaf_t[:, 2 * p + side : 2 * p + side + 1]
        leaf = jnp.where(parents == p, column, leaf)
    logits = margins + leaf
    top = jnp.max(logits, axis=0, keepdims=True)
    grown = jnp.exp(logits - top)
    prob = grown / jnp.sum(grown, axis=0, keepdims=True)
    classes = lax.broadcasted_iota(jnp.int32, margins.shape, 0)
    hot = jnp.where(classes == labels, 1.0, 0.0)
    return prob - hot, 2.0 * prob * (1.0 - prob)


def kernel(
    sf_hbm, sb_hbm, margin_hbm, label_hbm, bins_hbm, par_hbm, parrow_hbm, leaf_hbm,
    gain_ref, total_ref,
    sf_ref, sb_ref, margin_ref, label_ref, bins_ref, par_ref, parrow_ref, leaf_ref,
    bit_f32, bit_send, bit_recv, bin_send, bin_recv, bin_all, node_all, node_rel,
    spec, grads, acc, chunk_tot, group_tot, gain_send, gain_recv,
    in_sem, bit_ss, bit_rs, bin_ss, bin_rs, node_ss, node_rs, x_ss, x_rs,
    z_ss, z_rs, y_ss, y_rs, far_ss, far_rs, sib_ss, sib_rs, out_ss, out_rs,
    ct_ss, ct_rs, gt_ss, gt_rs,
):
    row = lax.axis_index("rows")
    feat = lax.axis_index("feat")
    y, core = row // 2, row % 2
    z, x = feat // 4, feat % 4
    odd = feat % 2

    def send(src, dst, ss, rs, r, f):
        return pltpu.make_async_remote_copy(
            src_ref=src, dst_ref=dst, send_sem=ss, recv_sem=rs,
            device_id=(r, f), device_id_type=MESH,
        )

    barrier = pltpu.get_barrier_semaphore()
    for d in FAR_FIRST:
        pl.semaphore_signal(barrier, inc=1, device_id=(row, (feat + d) % NF), device_id_type=MESH)
    for d in range(1, NR):
        pl.semaphore_signal(barrier, inc=1, device_id=((row + d) % NR, feat), device_id_type=MESH)

    inputs = [
        pltpu.make_async_copy(src, dst, in_sem.at[k])
        for k, (src, dst) in enumerate((
            (bins_hbm, bins_ref), (parrow_hbm, parrow_ref), (sf_hbm, sf_ref),
            (sb_hbm, sb_ref), (margin_hbm, margin_ref), (label_hbm, label_ref),
            (par_hbm, par_ref), (leaf_hbm, leaf_ref),
        ))
    ]
    for copy in inputs:
        copy.start()
    for copy in inputs:
        copy.wait()

    right = jnp.zeros((1, GROUP), F32)
    for p in range(PARENTS):
        local = sf_ref[p] - feat * FD
        owned = jnp.logical_and(local >= 0, local < FD).astype(jnp.int32)
        at = jnp.minimum(jnp.maximum(local, 0), FD - 1)
        limit = sb_ref[p] * owned + BINS * (1 - owned)
        hit = jnp.logical_and(bins_ref[pl.ds(at, 1), :] > limit, parrow_ref[...] == p)
        right = jnp.where(hit, 1.0, right)
    bit_f32[...] = jnp.zeros_like(bit_f32)
    for k in range(KB):
        bit_f32[k : k + 1, :] = right[:, k * LANES : (k + 1) * LANES]
    bit_send[...] = bit_f32[...].astype(BF)

    def arrange(value):
        padded = jnp.concatenate(
            [value, jnp.zeros((value.shape[0], 2 * LANES - OWN), value.dtype)], axis=1
        )
        turned = jnp.concatenate([padded[:, 64:], padded[:, :64]], axis=1)
        return jnp.where(odd == 1, turned, padded)

    def rows_of(ref, pair, side):
        main = ref[pl.ds(3 * pair + 2 * side, 1), :]
        rest = ref[pl.ds(3 * pair + 1, 1), :]
        return main, rest

    margins = arrange(margin_ref[...])
    labels = arrange(label_ref[...])
    own_parents = jnp.concatenate(rows_of(par_ref, feat // 2, odd), axis=1)
    leaf_t = leaf_ref[...].T
    first_half = lax.broadcasted_iota(jnp.int32, (CLASSES, LANES), 1) < 64
    keep = first_half == (odd == 0)
    for side in range(2):
        g, h = own_gradients(margins, labels, own_parents, leaf_t, side)
        rest = jnp.where(keep, g[:, LANES:], pltpu.roll(h[:, LANES:], 64, 1))
        spec[x, side] = jnp.concatenate([g[:, :LANES], h[:, :LANES], rest], axis=0).astype(BF)

    def load_bins(to):
        first = pl.multiple_of(to * FL, FL)
        return [
            bins_ref[pl.ds(first, FL), k * LANES : (k + 1) * LANES].astype(F32)
            for k in range(KB)
        ]

    def row_at(dy, other):
        return 2 * ((y + dy) % 4) + (core + other) % 2

    def bit_copy(d):
        return send(
            bit_send, bit_recv.at[d], bit_ss.at[d], bit_rs.at[d], row, (feat + d) % NF
        )

    def x_copy(d):
        at = spec.at[x]
        return send(at, at, x_ss.at[d], x_rs.at[d], row, 4 * z + (x + d) % 4)

    def bin_copy(d):
        to = row_at(*ROW_ORDER[d])
        return send(bin_send.at[d], bin_recv.at[d], bin_ss.at[d], bin_rs.at[d], to, feat)

    def node_copy(d):
        to = row_at(*ROW_ORDER[d])
        return send(node_all.at[row], node_all.at[row], node_ss.at[d], node_rs.at[d], to, feat)

    def arrived(at, sem):
        send(at, at, sem, sem, row, feat).wait_recv()

    def order(i):
        return i + i // 2 - 2 * (i // 3)

    def block(half, dz, dy):
        return grads.at[half, (z + dz) % 4, (y + dy) % 4]

    def z_copy(way):
        at = block(core, 0, 0)
        to = 4 * ((z + 1 + 2 * way) % 4) + x
        return send(at, at, z_ss.at[way], z_rs.at[way], row, to)

    def z_far_copy(way):
        at = block(core, 3 - 2 * way, 0).at[pl.ds(2 * way, 2)]
        to = 4 * ((z + 1 + 2 * way) % 4) + x
        return send(at, at, z_ss.at[2 + way], z_rs.at[2 + way], row, to)

    def y_copy(way, i):
        at = block(core, order(i), 0)
        return send(at, at, y_ss.at[way, i], y_rs.at[way, i], row_at(1 + 2 * way, 0), feat)

    def y_far_copy(i):
        way = i // 2
        at = block(core, order(i), 3 - 2 * way)
        return send(at, at, far_ss.at[i], far_rs.at[i], row_at(1 + 2 * way, 0), feat)

    def sib_copy(dy, i):
        at = block(core, order(i), dy)
        return send(at, at, sib_ss.at[dy, i], sib_rs.at[dy, i], row_at(0, 1), feat)

    def sib_wait(dy, i):
        arrived(block(1 - core, order(i), dy), sib_rs.at[dy, i])

    def pass_on(i):
        sib_copy(0, i).start()
        y_copy(0, i).start()
        y_copy(1, i).start()

    def y_arrival(i):
        for way in range(2):
            arrived(block(core, order(i), 3 - 2 * way), y_rs.at[way, i])
            if i // 2 == way:
                y_far_copy(i).start()
            sib_copy(3 - 2 * way, i).start()

    def far_arrival(i):
        arrived(block(core, order(i), 2), far_rs.at[i])
        sib_copy(2, i).start()

    def renumber(r):
        nodes = node_all[r] - (CHIP * (y + 1)).astype(F32)
        nodes = jnp.where(nodes < 0, nodes + NODES, nodes)
        node_rel[r] = jnp.where(nodes < 0, nodes + NODES, nodes)

    def row_arrival(d):
        bin_copy(d).wait_recv()
        dy, other = ROW_ORDER[d]
        came = row_at(4 - dy, other)
        part = bin_recv[d].astype(F32)
        for k in range(KB):
            bin_all[came, k] = part[k * FL : (k + 1) * FL]
        arrived(node_all.at[came], node_rs.at[d])
        renumber(came)

    pl.semaphore_wait(barrier, NF - 1 + NR - 1)
    for d in FAR_FIRST:
        bit_copy(d).start()
    for d in (1, 3, 2):
        x_copy(d).start()
    for d, (dy, other) in enumerate(ROW_ORDER):
        bin_send[d] = jnp.concatenate(load_bins(row_at(dy, other)), axis=0).astype(BF)
        bin_copy(d).start()
    for k, part in enumerate(load_bins(row)):
        bin_all[row, k] = part

    acc[...] = jnp.zeros_like(acc)

    bits = bit_send[...].astype(F32)
    for d in range(1, NF):
        bit_copy(d).wait_recv()
        bits = bits + bit_recv[d].astype(F32)
    node_all[row] = (2 * par_ref[...]).astype(F32) + bits[:KB]
    renumber(row)
    bit_f32[...] = bits
    for d in range(NR - 1):
        node_copy(d).start()

    for d in (1, 3, 2):
        arrived(spec.at[(x + 4 - d) % 4], x_rs.at[d])
    for xx in range(4):
        main, rest = rows_of(bit_f32, 2 * z + xx // 2, xx % 2)
        low = lax.broadcasted_iota(jnp.int32, (1, LANES), 1) < 64
        turned = jnp.concatenate([rest[:, 64:], rest[:, :64]], axis=1)
        rest = jnp.where(low, rest, turned) if xx % 2 == 0 else jnp.where(low, turned, rest)
        side = jnp.concatenate(
            [jnp.broadcast_to(main, (64, LANES)), jnp.broadcast_to(rest, (32, LANES))], axis=0
        ).astype(BF)
        grads[core, z, y, xx] = jnp.where(side > BF(0.5), spec[xx, 1], spec[xx, 0])
    sib_copy(0, 0).start()
    z_copy(0).start()
    z_copy(1).start()
    y_copy(0, 0).start()
    y_copy(1, 0).start()
    row_arrival(0)

    lane_low = lax.broadcasted_iota(jnp.int32, (32, LANES), 1) < 64
    bin_ids = lax.broadcasted_iota(jnp.int32, (BINS, LANES), 0).astype(F32).astype(BF)
    node_ids = lax.broadcasted_iota(jnp.int32, (NODES, LANES), 0).astype(F32).astype(BF)
    contract = (((1,), (1,)), ((), ()))

    def pair_pieces(half, zz, yy, q):
        even = grads[half, zz, yy, 2 * q]
        last = grads[half, zz, yy, 2 * q + 1]
        rest_e, rest_o = even[64:], last[64:]
        low = jnp.where(lane_low, rest_e, rest_o)
        high = jnp.where(lane_low, rest_o, rest_e).astype(F32)
        high = pltpu.roll(high, 64, 1).astype(BF)
        return even[:64], jnp.concatenate([low, high], axis=0), last[:64]

    def accumulate(blocks, low, high):
        weighted, masks = [], []
        for half, zz, yy in blocks:
            group = 2 * yy + half
            for q in range(2):
                first = 3 * (2 * zz + q)
                for i, piece in enumerate(pair_pieces(half, zz, yy, q)):
                    nodes = node_rel[group, pl.ds(first + i, 1), :].astype(BF)
                    wide = jnp.broadcast_to(nodes, (COLS, LANES))
                    zero = jnp.zeros_like(piece)
                    weighted.append(
                        jnp.concatenate(
                            [jnp.where(wide == BF(n), piece, zero) for n in range(low, high)],
                            axis=0,
                        )
                    )
                    rows = []
                    for f in range(FL):
                        here = bin_all[group, first + i, f : f + 1, :].astype(BF)
                        under = jnp.broadcast_to(here, (BINS, LANES)) <= bin_ids
                        rows.append(jnp.where(under, BF(1), BF(0)))
                    masks.append(jnp.concatenate(rows, axis=0))
        acc[low * COLS : high * COLS] += lax.dot_general(
            jnp.concatenate(weighted, axis=1),
            jnp.concatenate(masks, axis=1),
            contract,
            preferred_element_type=F32,
        )

    hots, pieces = [], []
    for q in range(2):
        for i, piece in enumerate(pair_pieces(core, z, y, q)):
            nodes = node_all[row, pl.ds(3 * (2 * z + q) + i, 1), :].astype(BF)
            same = jnp.broadcast_to(nodes, (NODES, LANES)) == node_ids
            hots.append(jnp.where(same, BF(1), BF(0)))
            pieces.append(piece)
    chunk_tot[z] = lax.dot_general(
        jnp.concatenate(hots, axis=1),
        jnp.concatenate(pieces, axis=1),
        contract,
        preferred_element_type=F32,
    )

    def chunk_tot_copy(d):
        at = chunk_tot.at[z]
        return send(at, at, ct_ss.at[d], ct_rs.at[d], row, 4 * ((z + d) % 4) + x)

    def group_tot_copy(d):
        at = group_tot.at[row]
        return send(at, at, gt_ss.at[d], gt_rs.at[d], row_at(*ROW_ORDER[d]), feat)

    for d in range(1, 4):
        chunk_tot_copy(d).start()

    def first(u, carry):
        @pl.when(u == 1)
        def _():
            sib_wait(0, 0)

        accumulate([((core + u) % 2, z, y)], 0, NODES)
        return carry

    lax.fori_loop(0, 2, first, 0)

    def near(u, carry):
        @pl.when(u == 0)
        def _():
            for way in range(2):
                arrived(block(core, 3 - 2 * way, 0), z_rs.at[way])
                z_far_copy(way).start()
            pass_on(1)
            pass_on(2)

        @pl.when(u == 1)
        def _():
            sib_wait(0, 1)
            sib_wait(0, 2)

        half = (core + u) % 2
        accumulate([(half, (z + 1) % 4, y), (half, (z + 3) % 4, y)], 0, NODES)
        return carry

    lax.fori_loop(0, 2, near, 0)

    for way in range(2):
        arrived(block(core, 2, 0).at[pl.ds(2 * way, 2)], z_rs.at[2 + way])
    pass_on(3)
    y_arrival(0)

    for d in range(1, NR - 1):
        row_arrival(d)

    for d in range(1, 4):
        arrived(chunk_tot.at[(z + 4 - d) % 4], ct_rs.at[d])
    group_tot[row] = (chunk_tot[0] + chunk_tot[1]) + (chunk_tot[2] + chunk_tot[3])
    for d in range(NR - 1):
        group_tot_copy(d).start()

    def beyond_blocks(s):
        far = s // 4
        blocks = []
        for j in range(4):
            dy = (1 - far) * (3 - 2 * (j % 2)) + 2 * far
            i = (1 - far) * s + far * (2 * (s - 4) + j % 2)
            blocks.append(((core + j // 2) % 2, (z + order(i)) % 4, (y + dy) % 4))
        return blocks

    def early(s, carry):
        @pl.when(s == 0)
        def _():
            y_arrival(1)
            sib_wait(3, 0)
            sib_wait(1, 0)

        @pl.when(s == 1)
        def _():
            y_arrival(2)
            sib_wait(3, 1)
            sib_wait(1, 1)

        accumulate(beyond_blocks(s), 0, NODES)
        return carry

    lax.fori_loop(0, 2, early, 0)

    sib_wait(0, 3)
    accumulate([(core, (z + 2) % 4, y), (1 - core, (z + 2) % 4, y)], 0, NODES)

    def late(s, carry):
        @pl.when(s == 2)
        def _():
            y_arrival(3)
            far_arrival(0)
            far_arrival(1)
            sib_wait(3, 2)
            sib_wait(1, 2)

        @pl.when(s == 3)
        def _():
            far_arrival(2)
            far_arrival(3)
            sib_wait(3, 3)
            sib_wait(1, 3)

        @pl.when(s == 4)
        def _():
            sib_wait(2, 0)
            sib_wait(2, 1)

        @pl.when(s == 5)
        def _():
            sib_wait(2, 2)
            sib_wait(2, 3)

        accumulate(beyond_blocks(s), 0, NODES - CHIP)
        return carry

    lax.fori_loop(2, 6, late, 0)

    def gains(low, high):
        for n in range(low, high):
            base = n * COLS
            gl = acc[base : base + CLASSES, :]
            hl = acc[base + CLASSES : base + COLS, :]
            whole_g = acc[base : base + CLASSES, BINS - 1 : BINS]
            whole_h = acc[base + CLASSES : base + COLS, BINS - 1 : BINS]
            gr = whole_g - gl
            hr = whole_h - hl
            score = (
                gl * gl / (hl + RIDGE)
                + gr * gr / (hr + RIDGE)
                - whole_g * whole_g / (whole_h + RIDGE)
            )
            gain = jnp.sum(score, axis=0, keepdims=True) * (1.0 / CLASSES)
            for k in range(4):
                at = (n % 2) * 4 + k
                gain_send[n // 2, at : at + 1, :] = gain[:, k * LANES : (k + 1) * LANES]

    def out_copy(pair):
        to = 2 * ((y + 1 + pair // 2) % 4) + pair % 2
        at = out_rs.at[2 * (pair // 2) + core]
        return send(gain_send.at[pair], gain_recv.at[row], out_ss.at[pair], at, to, feat)

    def out_sib_copy():
        at = gain_send.at[NR - 1 - core]
        return send(at, gain_recv.at[row], out_ss.at[NR - 1], out_rs.at[NR - 1], row_at(0, 1), feat)

    gains(0, NODES - CHIP)
    for pair in (2, 3, 0, 1, 4, 5):
        out_copy(pair).start()

    def rest(s, carry):
        accumulate(beyond_blocks(s), NODES - CHIP, NODES)
        return carry

    lax.fori_loop(2, 6, rest, 0)
    gains(NODES - CHIP, NODES)
    out_sib_copy().start()
    gain_recv[row] = gain_send[NR - 2 + core]

    for d in range(NR - 1):
        dy, other = ROW_ORDER[d]
        arrived(group_tot.at[row_at(4 - dy, other)], gt_rs.at[d])
    totals = group_tot[0]
    for r in range(1, NR):
        totals = totals + group_tot[r]
    total_ref[...] = totals

    for k in range(3):
        for other in range(2):
            came = 2 * ((y + 3 - k) % 4) + other
            arrived(gain_recv.at[came], out_rs.at[2 * k + other])
    arrived(gain_recv.at[row_at(0, 1)], out_rs.at[NR - 1])
    for r in range(NR):
        for n in range(2):
            tile = gain_recv[r, 4 * n : 4 * n + 4, :]
            for side in range(2):
                at = pl.ds(r * FL + side, 4, stride=2)
                gain_ref[n, at, :] = tile[:, side * BINS : (side + 1) * BINS]

    for d in range(1, NF):
        bit_copy(d).wait_send()
    for d in range(NR - 1):
        bin_copy(d).wait_send()
        node_copy(d).wait_send()
        group_tot_copy(d).wait_send()
    for pair in range(6):
        out_copy(pair).wait_send()
    out_sib_copy().wait_send()
    for d in range(1, 4):
        x_copy(d).wait_send()
        chunk_tot_copy(d).wait_send()
    for way in range(2):
        z_copy(way).wait_send()
        z_far_copy(way).wait_send()
    for i in range(4):
        y_copy(0, i).wait_send()
        y_copy(1, i).wait_send()
        y_far_copy(i).wait_send()
        for dy in range(4):
            sib_copy(dy, i).wait_send()


def body(margins, labels, row_bins, parents, split_feature, split_bin, leaf_values):
    vmem = pl.BlockSpec(memory_space=pltpu.VMEM)
    hbm = pl.BlockSpec(memory_space=pltpu.HBM)
    dma = pltpu.SemaphoreType.DMA
    return pl.pallas_call(
        kernel,
        out_shape=(
            jax.ShapeDtypeStruct((2, FD, BINS), F32),
            jax.ShapeDtypeStruct((NODES, COLS), F32),
        ),
        in_specs=[hbm] * 8,
        out_specs=(vmem, vmem),
        scratch_shapes=[
            pltpu.SMEM((PARENTS,), jnp.int32),
            pltpu.SMEM((PARENTS,), jnp.int32),
            pltpu.VMEM((CLASSES, OWN), F32),
            pltpu.VMEM((1, OWN), jnp.int32),
            pltpu.VMEM((FD, GROUP), jnp.int32),
            pltpu.VMEM((KB, LANES), jnp.int32),
            pltpu.VMEM((1, GROUP), jnp.int32),
            pltpu.VMEM((NODES, CLASSES), F32),
            pltpu.VMEM((32, LANES), F32),
            pltpu.VMEM((32, LANES), BF),
            pltpu.VMEM((NF, 32, LANES), BF),
            pltpu.VMEM((NR, KB * FL, LANES), BF),
            pltpu.VMEM((NR, KB * FL, LANES), BF),
            pltpu.VMEM((NR, KB, FL, LANES), F32),
            pltpu.VMEM((NR, KB, LANES), F32),
            pltpu.VMEM((NR, KB, LANES), F32),
            pltpu.VMEM((4, 2, 96, LANES), BF),
            pltpu.VMEM((2, 4, 4, 4, 96, LANES), BF),
            pltpu.VMEM((NODES * COLS, FL * BINS), F32),
            pltpu.VMEM((4, NODES, COLS), F32),
            pltpu.VMEM((NR, NODES, COLS), F32),
            pltpu.VMEM((NR, 8, LANES), F32),
            pltpu.VMEM((NR, 8, LANES), F32),
            dma((8,)),
            dma((NF,)), dma((NF,)), dma((NR,)), dma((NR,)), dma((NR,)), dma((NR,)),
            dma((4,)), dma((4,)), dma((4,)), dma((4,)),
            dma((2, 4)), dma((2, 4)), dma((4,)), dma((4,)), dma((4, 4)), dma((4, 4)),
            dma((NR,)), dma((NR,)),
            dma((4,)), dma((4,)), dma((NR,)), dma((NR,)),
        ],
        compiler_params=pltpu.CompilerParams(
            collective_id=0, has_side_effects=True, vmem_limit_bytes=48 << 20
        ),
    )(
        *(
            pltpu.with_memory_space_constraint(value, pltpu.HBM)
            for value in (
                split_feature,
                split_bin,
                margins.T,
                labels.reshape(1, OWN),
                row_bins,
                parents.reshape(KB, LANES),
                parents.reshape(1, GROUP),
                leaf_values,
            )
        )
    )


def solution(mesh):
    return jax.shard_map(
        body,
        mesh=mesh,
        in_specs=(
            P(("rows", "feat"), None),
            P(("rows", "feat")),
            P("feat", "rows"),
            P("rows"),
            P(),
            P(),
            P(),
        ),
        out_specs=(P("rows", "feat", None), P()),
        check_vma=False,
    )
```

```python
import jax
import jax.numpy as jnp
from jax import lax
from jax.experimental import pallas as pl
from jax.experimental.pallas import tpu as pltpu
from jax.sharding import PartitionSpec as P

MESH = pl.DeviceIdType.MESH
BINS = 64
NODES = 16
CLASSES = 32
COLS = 2 * CLASSES
PARENTS = 8
RIDGE = 1.0
LANES = 128
NR = 8
NF = 16
OWN = 192
GROUP = 3072
KB = GROUP // LANES
FD = 64
FL = FD // NR
FAR_FIRST = (10, 6, 14, 9, 11, 8, 2, 5, 7, 13, 15, 4, 12, 1, 3)
ROW_ORDER = ((0, 1), (1, 0), (1, 1), (3, 0), (3, 1), (2, 0), (2, 1))
CHIP = 4
BF = jnp.bfloat16
F32 = jnp.float32


def own_gradients(margins, labels, parents, leaf_t, side):
    leaf = jnp.zeros(margins.shape, F32)
    for p in range(PARENTS):
        column = leaf_t[:, 2 * p + side : 2 * p + side + 1]
        leaf = jnp.where(parents == p, column, leaf)
    logits = margins + leaf
    top = jnp.max(logits, axis=0, keepdims=True)
    grown = jnp.exp(logits - top)
    prob = grown / jnp.sum(grown, axis=0, keepdims=True)
    classes = lax.broadcasted_iota(jnp.int32, margins.shape, 0)
    hot = jnp.where(classes == labels, 1.0, 0.0)
    return prob - hot, 2.0 * prob * (1.0 - prob)


def kernel(
    sf_hbm, sb_hbm, margin_hbm, label_hbm, bins_hbm, par_hbm, parrow_hbm, leaf_hbm,
    gain_ref, total_ref,
    sf_ref, sb_ref, margin_ref, label_ref, bins_ref, par_ref, parrow_ref, leaf_ref,
    bit_f32, bit_send, bit_recv, bin_send, bin_recv, bin_all, node_all, node_rel,
    spec, grads, acc, chunk_tot, group_tot, gain_send, gain_recv,
    in_sem, bit_ss, bit_rs, bin_ss, bin_rs, node_ss, node_rs, x_ss, x_rs,
    z_ss, z_rs, y_ss, y_rs, far_ss, far_rs, sib_ss, sib_rs, out_ss, out_rs,
    ct_ss, ct_rs, gt_ss, gt_rs,
):
    row = lax.axis_index("rows")
    feat = lax.axis_index("feat")
    y, core = row // 2, row % 2
    z, x = feat // 4, feat % 4
    odd = feat % 2

    def send(src, dst, ss, rs, r, f):
        return pltpu.make_async_remote_copy(
            src_ref=src, dst_ref=dst, send_sem=ss, recv_sem=rs,
            device_id=(r, f), device_id_type=MESH,
        )

    barrier = pltpu.get_barrier_semaphore()
    for d in FAR_FIRST:
        pl.semaphore_signal(barrier, inc=1, device_id=(row, (feat + d) % NF), device_id_type=MESH)
    for d in range(1, NR):
        pl.semaphore_signal(barrier, inc=1, device_id=((row + d) % NR, feat), device_id_type=MESH)

    inputs = [
        pltpu.make_async_copy(src, dst, in_sem.at[k])
        for k, (src, dst) in enumerate((
            (bins_hbm, bins_ref), (parrow_hbm, parrow_ref), (sf_hbm, sf_ref),
            (sb_hbm, sb_ref), (margin_hbm, margin_ref), (label_hbm, label_ref),
            (par_hbm, par_ref), (leaf_hbm, leaf_ref),
        ))
    ]
    for copy in inputs:
        copy.start()
    for copy in inputs:
        copy.wait()

    right = jnp.zeros((1, GROUP), F32)
    for p in range(PARENTS):
        local = sf_ref[p] - feat * FD
        owned = jnp.logical_and(local >= 0, local < FD).astype(jnp.int32)
        at = jnp.minimum(jnp.maximum(local, 0), FD - 1)
        limit = sb_ref[p] * owned + BINS * (1 - owned)
        hit = jnp.logical_and(bins_ref[pl.ds(at, 1), :] > limit, parrow_ref[...] == p)
        right = jnp.where(hit, 1.0, right)
    bit_f32[...] = jnp.zeros_like(bit_f32)
    for k in range(KB):
        bit_f32[k : k + 1, :] = right[:, k * LANES : (k + 1) * LANES]
    bit_send[...] = bit_f32[...].astype(BF)

    def arrange(value):
        padded = jnp.concatenate(
            [value, jnp.zeros((value.shape[0], 2 * LANES - OWN), value.dtype)], axis=1
        )
        turned = jnp.concatenate([padded[:, 64:], padded[:, :64]], axis=1)
        return jnp.where(odd == 1, turned, padded)

    def rows_of(ref, pair, side):
        main = ref[pl.ds(3 * pair + 2 * side, 1), :]
        rest = ref[pl.ds(3 * pair + 1, 1), :]
        return main, rest

    margins = arrange(margin_ref[...])
    labels = arrange(label_ref[...])
    own_parents = jnp.concatenate(rows_of(par_ref, feat // 2, odd), axis=1)
    leaf_t = leaf_ref[...].T
    first_half = lax.broadcasted_iota(jnp.int32, (CLASSES, LANES), 1) < 64
    keep = first_half == (odd == 0)
    for side in range(2):
        g, h = own_gradients(margins, labels, own_parents, leaf_t, side)
        rest = jnp.where(keep, g[:, LANES:], pltpu.roll(h[:, LANES:], 64, 1))
        spec[x, side] = jnp.concatenate([g[:, :LANES], h[:, :LANES], rest], axis=0).astype(BF)

    def load_bins(to):
        first = pl.multiple_of(to * FL, FL)
        return [
            bins_ref[pl.ds(first, FL), k * LANES : (k + 1) * LANES].astype(F32)
            for k in range(KB)
        ]

    def row_at(dy, other):
        return 2 * ((y + dy) % 4) + (core + other) % 2

    def bit_copy(d):
        return send(
            bit_send, bit_recv.at[d], bit_ss.at[d], bit_rs.at[d], row, (feat + d) % NF
        )

    def x_copy(d):
        at = spec.at[x]
        return send(at, at, x_ss.at[d], x_rs.at[d], row, 4 * z + (x + d) % 4)

    def bin_copy(d):
        to = row_at(*ROW_ORDER[d])
        return send(bin_send.at[d], bin_recv.at[d], bin_ss.at[d], bin_rs.at[d], to, feat)

    def node_copy(d):
        to = row_at(*ROW_ORDER[d])
        return send(node_all.at[row], node_all.at[row], node_ss.at[d], node_rs.at[d], to, feat)

    def arrived(at, sem):
        send(at, at, sem, sem, row, feat).wait_recv()

    def order(i):
        return i + i // 2 - 2 * (i // 3)

    def block(half, dz, dy):
        return grads.at[half, (z + dz) % 4, (y + dy) % 4]

    def z_copy(way):
        at = block(core, 0, 0)
        to = 4 * ((z + 1 + 2 * way) % 4) + x
        return send(at, at, z_ss.at[way], z_rs.at[way], row, to)

    def z_far_copy(way):
        at = block(core, 3 - 2 * way, 0).at[pl.ds(2 * way, 2)]
        to = 4 * ((z + 1 + 2 * way) % 4) + x
        return send(at, at, z_ss.at[2 + way], z_rs.at[2 + way], row, to)

    def y_copy(way, i):
        at = block(core, order(i), 0)
        return send(at, at, y_ss.at[way, i], y_rs.at[way, i], row_at(1 + 2 * way, 0), feat)

    def y_far_copy(i):
        way = i // 2
        at = block(core, order(i), 3 - 2 * way)
        return send(at, at, far_ss.at[i], far_rs.at[i], row_at(1 + 2 * way, 0), feat)

    def sib_copy(dy, i):
        at = block(core, order(i), dy)
        return send(at, at, sib_ss.at[dy, i], sib_rs.at[dy, i], row_at(0, 1), feat)

    def sib_wait(dy, i):
        arrived(block(1 - core, order(i), dy), sib_rs.at[dy, i])

    def pass_on(i):
        sib_copy(0, i).start()
        y_copy(0, i).start()
        y_copy(1, i).start()

    def y_arrival(i):
        for way in range(2):
            arrived(block(core, order(i), 3 - 2 * way), y_rs.at[way, i])
            if i // 2 == way:
                y_far_copy(i).start()
            sib_copy(3 - 2 * way, i).start()

    def far_arrival(i):
        arrived(block(core, order(i), 2), far_rs.at[i])
        sib_copy(2, i).start()

    def renumber(r):
        nodes = node_all[r] - (CHIP * (y + 1)).astype(F32)
        nodes = jnp.where(nodes < 0, nodes + NODES, nodes)
        node_rel[r] = jnp.where(nodes < 0, nodes + NODES, nodes)

    def row_arrival(d):
        bin_copy(d).wait_recv()
        dy, other = ROW_ORDER[d]
        came = row_at(4 - dy, other)
        part = bin_recv[d].astype(F32)
        for k in range(KB):
            bin_all[came, k] = part[k * FL : (k + 1) * FL]
        arrived(node_all.at[came], node_rs.at[d])
        renumber(came)

    pl.semaphore_wait(barrier, NF - 1 + NR - 1)
    for d in FAR_FIRST:
        bit_copy(d).start()
    for d in (1, 3, 2):
        x_copy(d).start()
    for d, (dy, other) in enumerate(ROW_ORDER):
        bin_send[d] = jnp.concatenate(load_bins(row_at(dy, other)), axis=0).astype(BF)
        bin_copy(d).start()
    for k, part in enumerate(load_bins(row)):
        bin_all[row, k] = part

    acc[...] = jnp.zeros_like(acc)

    bits = bit_send[...].astype(F32)
    for d in range(1, NF):
        bit_copy(d).wait_recv()
        bits = bits + bit_recv[d].astype(F32)
    node_all[row] = (2 * par_ref[...]).astype(F32) + bits[:KB]
    renumber(row)
    bit_f32[...] = bits
    for d in range(NR - 1):
        node_copy(d).start()

    for d in (1, 3, 2):
        arrived(spec.at[(x + 4 - d) % 4], x_rs.at[d])
    for xx in range(4):
        main, rest = rows_of(bit_f32, 2 * z + xx // 2, xx % 2)
        low = lax.broadcasted_iota(jnp.int32, (1, LANES), 1) < 64
        turned = jnp.concatenate([rest[:, 64:], rest[:, :64]], axis=1)
        rest = jnp.where(low, rest, turned) if xx % 2 == 0 else jnp.where(low, turned, rest)
        side = jnp.concatenate(
            [jnp.broadcast_to(main, (64, LANES)), jnp.broadcast_to(rest, (32, LANES))], axis=0
        ).astype(BF)
        grads[core, z, y, xx] = jnp.where(side > BF(0.5), spec[xx, 1], spec[xx, 0])
    sib_copy(0, 0).start()
    z_copy(0).start()
    z_copy(1).start()
    y_copy(0, 0).start()
    y_copy(1, 0).start()
    row_arrival(0)

    lane_low = lax.broadcasted_iota(jnp.int32, (32, LANES), 1) < 64
    bin_ids = lax.broadcasted_iota(jnp.int32, (BINS, LANES), 0).astype(F32).astype(BF)
    node_ids = lax.broadcasted_iota(jnp.int32, (NODES, LANES), 0).astype(F32).astype(BF)
    contract = (((1,), (1,)), ((), ()))

    def pair_pieces(half, zz, yy, q):
        even = grads[half, zz, yy, 2 * q]
        last = grads[half, zz, yy, 2 * q + 1]
        rest_e, rest_o = even[64:], last[64:]
        low = jnp.where(lane_low, rest_e, rest_o)
        high = jnp.where(lane_low, rest_o, rest_e).astype(F32)
        high = pltpu.roll(high, 64, 1).astype(BF)
        return even[:64], jnp.concatenate([low, high], axis=0), last[:64]

    def accumulate(blocks, low, high):
        weighted, masks = [], []
        for half, zz, yy in blocks:
            group = 2 * yy + half
            for q in range(2):
                first = 3 * (2 * zz + q)
                for i, piece in enumerate(pair_pieces(half, zz, yy, q)):
                    nodes = node_rel[group, pl.ds(first + i, 1), :].astype(BF)
                    wide = jnp.broadcast_to(nodes, (COLS, LANES))
                    zero = jnp.zeros_like(piece)
                    weighted.append(
                        jnp.concatenate(
                            [jnp.where(wide == BF(n), piece, zero) for n in range(low, high)],
                            axis=0,
                        )
                    )
                    rows = []
                    for f in range(FL):
                        here = bin_all[group, first + i, f : f + 1, :].astype(BF)
                        under = jnp.broadcast_to(here, (BINS, LANES)) <= bin_ids
                        rows.append(jnp.where(under, BF(1), BF(0)))
                    masks.append(jnp.concatenate(rows, axis=0))
        acc[low * COLS : high * COLS] += lax.dot_general(
            jnp.concatenate(weighted, axis=1),
            jnp.concatenate(masks, axis=1),
            contract,
            preferred_element_type=F32,
        )

    hots, pieces = [], []
    for q in range(2):
        for i, piece in enumerate(pair_pieces(core, z, y, q)):
            nodes = node_all[row, pl.ds(3 * (2 * z + q) + i, 1), :].astype(BF)
            same = jnp.broadcast_to(nodes, (NODES, LANES)) == node_ids
            hots.append(jnp.where(same, BF(1), BF(0)))
            pieces.append(piece)
    chunk_tot[z] = lax.dot_general(
        jnp.concatenate(hots, axis=1),
        jnp.concatenate(pieces, axis=1),
        contract,
        preferred_element_type=F32,
    )

    def chunk_tot_copy(d):
        at = chunk_tot.at[z]
        return send(at, at, ct_ss.at[d], ct_rs.at[d], row, 4 * ((z + d) % 4) + x)

    def group_tot_copy(d):
        at = group_tot.at[row]
        return send(at, at, gt_ss.at[d], gt_rs.at[d], row_at(*ROW_ORDER[d]), feat)

    for d in range(1, 4):
        chunk_tot_copy(d).start()

    def first(u, carry):
        @pl.when(u == 1)
        def _():
            sib_wait(0, 0)

        accumulate([((core + u) % 2, z, y)], 0, NODES)
        return carry

    lax.fori_loop(0, 2, first, 0)

    def near(u, carry):
        @pl.when(u == 0)
        def _():
            for way in range(2):
                arrived(block(core, 3 - 2 * way, 0), z_rs.at[way])
                z_far_copy(way).start()
            pass_on(1)
            pass_on(2)

        @pl.when(u == 1)
        def _():
            y_arrival(0)
            sib_wait(0, 1)
            sib_wait(0, 2)

        half = (core + u) % 2
        accumulate([(half, (z + 1) % 4, y), (half, (z + 3) % 4, y)], 0, NODES)
        return carry

    lax.fori_loop(0, 2, near, 0)

    for way in range(2):
        arrived(block(core, 2, 0).at[pl.ds(2 * way, 2)], z_rs.at[2 + way])
    pass_on(3)

    for d in range(1, NR - 1):
        row_arrival(d)

    for d in range(1, 4):
        arrived(chunk_tot.at[(z + 4 - d) % 4], ct_rs.at[d])
    group_tot[row] = (chunk_tot[0] + chunk_tot[1]) + (chunk_tot[2] + chunk_tot[3])
    for d in range(NR - 1):
        group_tot_copy(d).start()

    def other_y(half, k):
        far = k // 4
        blocks = []
        for j in range(2):
            dy = (1 - far) * (3 - 2 * j) + 2 * far
            i = (1 - far) * k + far * (2 * (k - 4) + j)
            blocks.append((half, (z + order(i)) % 4, (y + dy) % 4))
        return blocks

    def step_blocks(k):
        return other_y(core, k) + other_y(1 - core, k - 1)

    sib_wait(3, 0)
    sib_wait(1, 0)
    accumulate(other_y(core, 0) + other_y(1 - core, 0), 0, NODES)

    y_arrival(1)
    sib_wait(0, 3)
    last_z = [(core, (z + 2) % 4, y), (1 - core, (z + 2) % 4, y)]
    accumulate(other_y(core, 1) + last_z, 0, NODES)

    def late(k, carry):
        @pl.when(k == 2)
        def _():
            y_arrival(2)
            sib_wait(3, 1)
            sib_wait(1, 1)

        @pl.when(k == 3)
        def _():
            y_arrival(3)
            sib_wait(3, 2)
            sib_wait(1, 2)

        @pl.when(k == 4)
        def _():
            far_arrival(0)
            far_arrival(1)
            sib_wait(3, 3)
            sib_wait(1, 3)

        @pl.when(k == 5)
        def _():
            far_arrival(2)
            far_arrival(3)
            sib_wait(2, 0)
            sib_wait(2, 1)

        accumulate(step_blocks(k), 0, NODES - CHIP)
        return carry

    lax.fori_loop(2, 6, late, 0)

    sib_wait(2, 2)
    sib_wait(2, 3)
    accumulate(other_y(1 - core, 5), 0, NODES)

    def gains(low, high):
        for n in range(low, high):
            base = n * COLS
            gl = acc[base : base + CLASSES, :]
            hl = acc[base + CLASSES : base + COLS, :]
            whole_g = acc[base : base + CLASSES, BINS - 1 : BINS]
            whole_h = acc[base + CLASSES : base + COLS, BINS - 1 : BINS]
            gr = whole_g - gl
            hr = whole_h - hl
            score = (
                gl * gl / (hl + RIDGE)
                + gr * gr / (hr + RIDGE)
                - whole_g * whole_g / (whole_h + RIDGE)
            )
            gain = jnp.sum(score, axis=0, keepdims=True) * (1.0 / CLASSES)
            for k in range(4):
                at = (n % 2) * 4 + k
                gain_send[n // 2, at : at + 1, :] = gain[:, k * LANES : (k + 1) * LANES]

    def out_copy(pair):
        to = 2 * ((y + 1 + pair // 2) % 4) + pair % 2
        at = out_rs.at[2 * (pair // 2) + core]
        return send(gain_send.at[pair], gain_recv.at[row], out_ss.at[pair], at, to, feat)

    def out_sib_copy():
        at = gain_send.at[NR - 1 - core]
        return send(at, gain_recv.at[row], out_ss.at[NR - 1], out_rs.at[NR - 1], row_at(0, 1), feat)

    gains(0, NODES - CHIP)
    for pair in (2, 3, 0, 1, 4, 5):
        out_copy(pair).start()

    def rest(k, carry):
        accumulate(step_blocks(k), NODES - CHIP, NODES)
        return carry

    lax.fori_loop(2, 6, rest, 0)
    gains(NODES - CHIP, NODES)
    out_sib_copy().start()
    gain_recv[row] = gain_send[NR - 2 + core]

    for d in range(NR - 1):
        dy, other = ROW_ORDER[d]
        arrived(group_tot.at[row_at(4 - dy, other)], gt_rs.at[d])
    totals = group_tot[0]
    for r in range(1, NR):
        totals = totals + group_tot[r]
    total_ref[...] = totals

    for k in range(3):
        for other in range(2):
            came = 2 * ((y + 3 - k) % 4) + other
            arrived(gain_recv.at[came], out_rs.at[2 * k + other])
    arrived(gain_recv.at[row_at(0, 1)], out_rs.at[NR - 1])
    for r in range(NR):
        for n in range(2):
            tile = gain_recv[r, 4 * n : 4 * n + 4, :]
            for side in range(2):
                at = pl.ds(r * FL + side, 4, stride=2)
                gain_ref[n, at, :] = tile[:, side * BINS : (side + 1) * BINS]

    for d in range(1, NF):
        bit_copy(d).wait_send()
    for d in range(NR - 1):
        bin_copy(d).wait_send()
        node_copy(d).wait_send()
        group_tot_copy(d).wait_send()
    for pair in range(6):
        out_copy(pair).wait_send()
    out_sib_copy().wait_send()
    for d in range(1, 4):
        x_copy(d).wait_send()
        chunk_tot_copy(d).wait_send()
    for way in range(2):
        z_copy(way).wait_send()
        z_far_copy(way).wait_send()
    for i in range(4):
        y_copy(0, i).wait_send()
        y_copy(1, i).wait_send()
        y_far_copy(i).wait_send()
        for dy in range(4):
            sib_copy(dy, i).wait_send()


def body(margins, labels, row_bins, parents, split_feature, split_bin, leaf_values):
    vmem = pl.BlockSpec(memory_space=pltpu.VMEM)
    hbm = pl.BlockSpec(memory_space=pltpu.HBM)
    dma = pltpu.SemaphoreType.DMA
    return pl.pallas_call(
        kernel,
        out_shape=(
            jax.ShapeDtypeStruct((2, FD, BINS), F32),
            jax.ShapeDtypeStruct((NODES, COLS), F32),
        ),
        in_specs=[hbm] * 8,
        out_specs=(vmem, vmem),
        scratch_shapes=[
            pltpu.SMEM((PARENTS,), jnp.int32),
            pltpu.SMEM((PARENTS,), jnp.int32),
            pltpu.VMEM((CLASSES, OWN), F32),
            pltpu.VMEM((1, OWN), jnp.int32),
            pltpu.VMEM((FD, GROUP), jnp.int32),
            pltpu.VMEM((KB, LANES), jnp.int32),
            pltpu.VMEM((1, GROUP), jnp.int32),
            pltpu.VMEM((NODES, CLASSES), F32),
            pltpu.VMEM((32, LANES), F32),
            pltpu.VMEM((32, LANES), BF),
            pltpu.VMEM((NF, 32, LANES), BF),
            pltpu.VMEM((NR, KB * FL, LANES), BF),
            pltpu.VMEM((NR, KB * FL, LANES), BF),
            pltpu.VMEM((NR, KB, FL, LANES), F32),
            pltpu.VMEM((NR, KB, LANES), F32),
            pltpu.VMEM((NR, KB, LANES), F32),
            pltpu.VMEM((4, 2, 96, LANES), BF),
            pltpu.VMEM((2, 4, 4, 4, 96, LANES), BF),
            pltpu.VMEM((NODES * COLS, FL * BINS), F32),
            pltpu.VMEM((4, NODES, COLS), F32),
            pltpu.VMEM((NR, NODES, COLS), F32),
            pltpu.VMEM((NR, 8, LANES), F32),
            pltpu.VMEM((NR, 8, LANES), F32),
            dma((8,)),
            dma((NF,)), dma((NF,)), dma((NR,)), dma((NR,)), dma((NR,)), dma((NR,)),
            dma((4,)), dma((4,)), dma((4,)), dma((4,)),
            dma((2, 4)), dma((2, 4)), dma((4,)), dma((4,)), dma((4, 4)), dma((4, 4)),
            dma((NR,)), dma((NR,)),
            dma((4,)), dma((4,)), dma((NR,)), dma((NR,)),
        ],
        compiler_params=pltpu.CompilerParams(
            collective_id=0, has_side_effects=True, vmem_limit_bytes=48 << 20
        ),
    )(
        *(
            pltpu.with_memory_space_constraint(value, pltpu.HBM)
            for value in (
                split_feature,
                split_bin,
                margins.T,
                labels.reshape(1, OWN),
                row_bins,
                parents.reshape(KB, LANES),
                parents.reshape(1, GROUP),
                leaf_values,
            )
        )
    )


def solution(mesh):
    return jax.shard_map(
        body,
        mesh=mesh,
        in_specs=(
            P(("rows", "feat"), None),
            P(("rows", "feat")),
            P("feat", "rows"),
            P("rows"),
            P(),
            P(),
            P(),
        ),
        out_specs=(P("rows", "feat", None), P()),
        check_vma=False,
    )
```

```python
import jax
import jax.numpy as jnp
from jax import lax
from jax.experimental import pallas as pl
from jax.experimental.pallas import tpu as pltpu
from jax.sharding import PartitionSpec as P

MESH = pl.DeviceIdType.MESH
BINS = 64
NODES = 16
CLASSES = 32
COLS = 2 * CLASSES
PARENTS = 8
RIDGE = 1.0
LANES = 128
NR = 8
NF = 16
OWN = 192
GROUP = 3072
KB = GROUP // LANES
FD = 64
FL = FD // NR
FAR_FIRST = (10, 6, 14, 9, 11, 8, 2, 5, 7, 13, 15, 4, 12, 1, 3)
ROW_ORDER = ((0, 1), (1, 0), (1, 1), (3, 0), (3, 1), (2, 0), (2, 1))
CHIP = 4
BF = jnp.bfloat16
F32 = jnp.float32


def own_gradients(margins, labels, parents, leaf_t, side):
    leaf = jnp.zeros(margins.shape, F32)
    for p in range(PARENTS):
        column = leaf_t[:, 2 * p + side : 2 * p + side + 1]
        leaf = jnp.where(parents == p, column, leaf)
    logits = margins + leaf
    top = jnp.max(logits, axis=0, keepdims=True)
    grown = jnp.exp(logits - top)
    prob = grown / jnp.sum(grown, axis=0, keepdims=True)
    classes = lax.broadcasted_iota(jnp.int32, margins.shape, 0)
    hot = jnp.where(classes == labels, 1.0, 0.0)
    return prob - hot, 2.0 * prob * (1.0 - prob)


def kernel(
    sf_hbm, sb_hbm, margin_hbm, label_hbm, bins_hbm, par_hbm, parrow_hbm, leaf_hbm,
    gain_ref, total_ref,
    sf_ref, sb_ref, margin_ref, label_ref, bins_ref, par_ref, parrow_ref, leaf_ref,
    bit_f32, bit_send, bit_recv, bin_send, bin_recv, bin_all, node_all, node_rel,
    spec, grads, acc, chunk_tot, group_tot, gain_send, gain_recv,
    in_sem, bit_ss, bit_rs, bin_ss, bin_rs, node_ss, node_rs, x_ss, x_rs,
    z_ss, z_rs, y_ss, y_rs, far_ss, far_rs, sib_ss, sib_rs, out_ss, out_rs,
    ct_ss, ct_rs, gt_ss, gt_rs, y_ready,
):
    row = lax.axis_index("rows")
    feat = lax.axis_index("feat")
    y, core = row // 2, row % 2
    z, x = feat // 4, feat % 4
    odd = feat % 2

    def send(src, dst, ss, rs, r, f):
        return pltpu.make_async_remote_copy(
            src_ref=src, dst_ref=dst, send_sem=ss, recv_sem=rs,
            device_id=(r, f), device_id_type=MESH,
        )

    barrier = pltpu.get_barrier_semaphore()
    for d in FAR_FIRST:
        pl.semaphore_signal(barrier, inc=1, device_id=(row, (feat + d) % NF), device_id_type=MESH)
    pl.semaphore_signal(
        barrier, inc=1, device_id=(row + 1 - 2 * core, feat), device_id_type=MESH
    )

    def rank(yy):
        return yy + yy // 2 - 2 * (yy // 3)

    def greet_y(sem, up):
        for dy in range(1, 4):
            there = (y + dy) % 4
            ahead = rank(there) > rank(y) if up else rank(there) < rank(y)
            for c in range(2):

                @pl.when(ahead)
                def _():
                    pl.semaphore_signal(
                        sem, inc=1, device_id=(2 * there + c, feat), device_id_type=MESH
                    )

    greet_y(barrier, True)

    inputs = [
        pltpu.make_async_copy(src, dst, in_sem.at[k])
        for k, (src, dst) in enumerate((
            (bins_hbm, bins_ref), (parrow_hbm, parrow_ref), (sf_hbm, sf_ref),
            (sb_hbm, sb_ref), (margin_hbm, margin_ref), (label_hbm, label_ref),
            (par_hbm, par_ref), (leaf_hbm, leaf_ref),
        ))
    ]
    for copy in inputs:
        copy.start()
    for copy in inputs:
        copy.wait()

    right = jnp.zeros((1, GROUP), F32)
    for p in range(PARENTS):
        local = sf_ref[p] - feat * FD
        owned = jnp.logical_and(local >= 0, local < FD).astype(jnp.int32)
        at = jnp.minimum(jnp.maximum(local, 0), FD - 1)
        limit = sb_ref[p] * owned + BINS * (1 - owned)
        hit = jnp.logical_and(bins_ref[pl.ds(at, 1), :] > limit, parrow_ref[...] == p)
        right = jnp.where(hit, 1.0, right)
    bit_f32[...] = jnp.zeros_like(bit_f32)
    for k in range(KB):
        bit_f32[k : k + 1, :] = right[:, k * LANES : (k + 1) * LANES]
    bit_send[...] = bit_f32[...].astype(BF)

    def arrange(value):
        padded = jnp.concatenate(
            [value, jnp.zeros((value.shape[0], 2 * LANES - OWN), value.dtype)], axis=1
        )
        turned = jnp.concatenate([padded[:, 64:], padded[:, :64]], axis=1)
        return jnp.where(odd == 1, turned, padded)

    def rows_of(ref, pair, side):
        main = ref[pl.ds(3 * pair + 2 * side, 1), :]
        rest = ref[pl.ds(3 * pair + 1, 1), :]
        return main, rest

    margins = arrange(margin_ref[...])
    labels = arrange(label_ref[...])
    own_parents = jnp.concatenate(rows_of(par_ref, feat // 2, odd), axis=1)
    leaf_t = leaf_ref[...].T
    first_half = lax.broadcasted_iota(jnp.int32, (CLASSES, LANES), 1) < 64
    keep = first_half == (odd == 0)
    for side in range(2):
        g, h = own_gradients(margins, labels, own_parents, leaf_t, side)
        rest = jnp.where(keep, g[:, LANES:], pltpu.roll(h[:, LANES:], 64, 1))
        spec[x, side] = jnp.concatenate([g[:, :LANES], h[:, :LANES], rest], axis=0).astype(BF)

    def load_bins(to):
        first = pl.multiple_of(to * FL, FL)
        return [
            bins_ref[pl.ds(first, FL), k * LANES : (k + 1) * LANES].astype(F32)
            for k in range(KB)
        ]

    def row_at(dy, other):
        return 2 * ((y + dy) % 4) + (core + other) % 2

    def bit_copy(d):
        return send(
            bit_send, bit_recv.at[d], bit_ss.at[d], bit_rs.at[d], row, (feat + d) % NF
        )

    def x_copy(d):
        at = spec.at[x]
        return send(at, at, x_ss.at[d], x_rs.at[d], row, 4 * z + (x + d) % 4)

    def bin_copy(d):
        to = row_at(*ROW_ORDER[d])
        return send(bin_send.at[d], bin_recv.at[d], bin_ss.at[d], bin_rs.at[d], to, feat)

    def node_copy(d):
        to = row_at(*ROW_ORDER[d])
        return send(node_all.at[row], node_all.at[row], node_ss.at[d], node_rs.at[d], to, feat)

    def arrived(at, sem):
        send(at, at, sem, sem, row, feat).wait_recv()

    def order(i):
        return i + i // 2 - 2 * (i // 3)

    def block(half, dz, dy):
        return grads.at[half, (z + dz) % 4, (y + dy) % 4]

    def z_copy(way):
        at = block(core, 0, 0)
        to = 4 * ((z + 1 + 2 * way) % 4) + x
        return send(at, at, z_ss.at[way], z_rs.at[way], row, to)

    def z_far_copy(way):
        at = block(core, 3 - 2 * way, 0).at[pl.ds(2 * way, 2)]
        to = 4 * ((z + 1 + 2 * way) % 4) + x
        return send(at, at, z_ss.at[2 + way], z_rs.at[2 + way], row, to)

    def y_copy(way, i):
        at = block(core, order(i), 0)
        return send(at, at, y_ss.at[way, i], y_rs.at[way, i], row_at(1 + 2 * way, 0), feat)

    def y_far_copy(i):
        way = i // 2
        at = block(core, order(i), 3 - 2 * way)
        return send(at, at, far_ss.at[i], far_rs.at[i], row_at(1 + 2 * way, 0), feat)

    def sib_copy(dy, i):
        at = block(core, order(i), dy)
        return send(at, at, sib_ss.at[dy, i], sib_rs.at[dy, i], row_at(0, 1), feat)

    def sib_wait(dy, i):
        arrived(block(1 - core, order(i), dy), sib_rs.at[dy, i])

    def pass_on(i):
        sib_copy(0, i).start()
        y_copy(0, i).start()
        y_copy(1, i).start()

    def y_arrival(i):
        for way in range(2):
            arrived(block(core, order(i), 3 - 2 * way), y_rs.at[way, i])
            if i // 2 == way:
                y_far_copy(i).start()
            sib_copy(3 - 2 * way, i).start()

    def far_arrival(i):
        arrived(block(core, order(i), 2), far_rs.at[i])
        sib_copy(2, i).start()

    def renumber(r):
        nodes = node_all[r] - (CHIP * (y + 1)).astype(F32)
        nodes = jnp.where(nodes < 0, nodes + NODES, nodes)
        node_rel[r] = jnp.where(nodes < 0, nodes + NODES, nodes)

    def row_arrival(d):
        bin_copy(d).wait_recv()
        dy, other = ROW_ORDER[d]
        came = row_at(4 - dy, other)
        part = bin_recv[d].astype(F32)
        for k in range(KB):
            bin_all[came, k] = part[k * FL : (k + 1) * FL]
        arrived(node_all.at[came], node_rs.at[d])
        renumber(came)

    pl.semaphore_wait(barrier, NF + 2 * rank(y))
    greet_y(y_ready, False)
    for d in FAR_FIRST:
        bit_copy(d).start()
    for d in (1, 3, 2):
        x_copy(d).start()

    @pl.when(rank(y) < 3)
    def _():
        pl.semaphore_wait(y_ready, 2 * (3 - rank(y)))

    for d, (dy, other) in enumerate(ROW_ORDER):
        bin_send[d] = jnp.concatenate(load_bins(row_at(dy, other)), axis=0).astype(BF)
        bin_copy(d).start()
    for k, part in enumerate(load_bins(row)):
        bin_all[row, k] = part

    acc[...] = jnp.zeros_like(acc)

    bits = bit_send[...].astype(F32)
    for d in range(1, NF):
        bit_copy(d).wait_recv()
        bits = bits + bit_recv[d].astype(F32)
    node_all[row] = (2 * par_ref[...]).astype(F32) + bits[:KB]
    renumber(row)
    bit_f32[...] = bits
    for d in range(NR - 1):
        node_copy(d).start()

    for d in (1, 3, 2):
        arrived(spec.at[(x + 4 - d) % 4], x_rs.at[d])
    for xx in range(4):
        main, rest = rows_of(bit_f32, 2 * z + xx // 2, xx % 2)
        low = lax.broadcasted_iota(jnp.int32, (1, LANES), 1) < 64
        turned = jnp.concatenate([rest[:, 64:], rest[:, :64]], axis=1)
        rest = jnp.where(low, rest, turned) if xx % 2 == 0 else jnp.where(low, turned, rest)
        side = jnp.concatenate(
            [jnp.broadcast_to(main, (64, LANES)), jnp.broadcast_to(rest, (32, LANES))], axis=0
        ).astype(BF)
        grads[core, z, y, xx] = jnp.where(side > BF(0.5), spec[xx, 1], spec[xx, 0])
    sib_copy(0, 0).start()
    z_copy(0).start()
    z_copy(1).start()
    y_copy(0, 0).start()
    y_copy(1, 0).start()
    row_arrival(0)

    lane_low = lax.broadcasted_iota(jnp.int32, (32, LANES), 1) < 64
    bin_ids = lax.broadcasted_iota(jnp.int32, (BINS, LANES), 0).astype(F32).astype(BF)
    node_ids = lax.broadcasted_iota(jnp.int32, (NODES, LANES), 0).astype(F32).astype(BF)
    contract = (((1,), (1,)), ((), ()))

    def pair_pieces(half, zz, yy, q):
        even = grads[half, zz, yy, 2 * q]
        last = grads[half, zz, yy, 2 * q + 1]
        rest_e, rest_o = even[64:], last[64:]
        low = jnp.where(lane_low, rest_e, rest_o)
        high = jnp.where(lane_low, rest_o, rest_e).astype(F32)
        high = pltpu.roll(high, 64, 1).astype(BF)
        return even[:64], jnp.concatenate([low, high], axis=0), last[:64]

    def accumulate(blocks, low, high):
        weighted, masks = [], []
        for half, zz, yy in blocks:
            group = 2 * yy + half
            for q in range(2):
                first = 3 * (2 * zz + q)
                for i, piece in enumerate(pair_pieces(half, zz, yy, q)):
                    nodes = node_rel[group, pl.ds(first + i, 1), :].astype(BF)
                    wide = jnp.broadcast_to(nodes, (COLS, LANES))
                    zero = jnp.zeros_like(piece)
                    weighted.append(
                        jnp.concatenate(
                            [jnp.where(wide == BF(n), piece, zero) for n in range(low, high)],
                            axis=0,
                        )
                    )
                    rows = []
                    for f in range(FL):
                        here = bin_all[group, first + i, f : f + 1, :].astype(BF)
                        under = jnp.broadcast_to(here, (BINS, LANES)) <= bin_ids
                        rows.append(jnp.where(under, BF(1), BF(0)))
                    masks.append(jnp.concatenate(rows, axis=0))
        acc[low * COLS : high * COLS] += lax.dot_general(
            jnp.concatenate(weighted, axis=1),
            jnp.concatenate(masks, axis=1),
            contract,
            preferred_element_type=F32,
        )

    hots, pieces = [], []
    for q in range(2):
        for i, piece in enumerate(pair_pieces(core, z, y, q)):
            nodes = node_all[row, pl.ds(3 * (2 * z + q) + i, 1), :].astype(BF)
            same = jnp.broadcast_to(nodes, (NODES, LANES)) == node_ids
            hots.append(jnp.where(same, BF(1), BF(0)))
            pieces.append(piece)
    chunk_tot[z] = lax.dot_general(
        jnp.concatenate(hots, axis=1),
        jnp.concatenate(pieces, axis=1),
        contract,
        preferred_element_type=F32,
    )

    def chunk_tot_copy(d):
        at = chunk_tot.at[z]
        return send(at, at, ct_ss.at[d], ct_rs.at[d], row, 4 * ((z + d) % 4) + x)

    def group_tot_copy(d):
        at = group_tot.at[row]
        return send(at, at, gt_ss.at[d], gt_rs.at[d], row_at(*ROW_ORDER[d]), feat)

    for d in range(1, 4):
        chunk_tot_copy(d).start()

    def first(u, carry):
        @pl.when(u == 1)
        def _():
            sib_wait(0, 0)

        accumulate([((core + u) % 2, z, y)], 0, NODES)
        return carry

    lax.fori_loop(0, 2, first, 0)

    def near(u, carry):
        @pl.when(u == 0)
        def _():
            for way in range(2):
                arrived(block(core, 3 - 2 * way, 0), z_rs.at[way])
                z_far_copy(way).start()
            pass_on(1)
            pass_on(2)

        @pl.when(u == 1)
        def _():
            y_arrival(0)
            sib_wait(0, 1)
            sib_wait(0, 2)

        half = (core + u) % 2
        accumulate([(half, (z + 1) % 4, y), (half, (z + 3) % 4, y)], 0, NODES)
        return carry

    lax.fori_loop(0, 2, near, 0)

    for way in range(2):
        arrived(block(core, 2, 0).at[pl.ds(2 * way, 2)], z_rs.at[2 + way])
    pass_on(3)

    for d in range(1, NR - 1):
        row_arrival(d)

    for d in range(1, 4):
        arrived(chunk_tot.at[(z + 4 - d) % 4], ct_rs.at[d])
    group_tot[row] = (chunk_tot[0] + chunk_tot[1]) + (chunk_tot[2] + chunk_tot[3])
    for d in range(NR - 1):
        group_tot_copy(d).start()

    def other_y(half, k):
        far = k // 4
        blocks = []
        for j in range(2):
            dy = (1 - far) * (3 - 2 * j) + 2 * far
            i = (1 - far) * k + far * (2 * (k - 4) + j)
            blocks.append((half, (z + order(i)) % 4, (y + dy) % 4))
        return blocks

    def step_blocks(k):
        return other_y(core, k) + other_y(1 - core, k - 1)

    sib_wait(3, 0)
    sib_wait(1, 0)
    accumulate(other_y(core, 0) + other_y(1 - core, 0), 0, NODES)

    y_arrival(1)
    sib_wait(0, 3)
    last_z = [(core, (z + 2) % 4, y), (1 - core, (z + 2) % 4, y)]
    accumulate(other_y(core, 1) + last_z, 0, NODES)

    def late(k, carry):
        @pl.when(k == 2)
        def _():
            y_arrival(2)
            sib_wait(3, 1)
            sib_wait(1, 1)

        @pl.when(k == 3)
        def _():
            y_arrival(3)
            sib_wait(3, 2)
            sib_wait(1, 2)

        @pl.when(k == 4)
        def _():
            far_arrival(0)
            far_arrival(1)
            sib_wait(3, 3)
            sib_wait(1, 3)

        @pl.when(k == 5)
        def _():
            far_arrival(2)
            far_arrival(3)
            sib_wait(2, 0)
            sib_wait(2, 1)

        accumulate(step_blocks(k), 0, NODES - CHIP)
        return carry

    lax.fori_loop(2, 6, late, 0)

    sib_wait(2, 2)
    sib_wait(2, 3)
    accumulate(other_y(1 - core, 5), 0, NODES)

    def gains(low, high):
        for n in range(low, high):
            base = n * COLS
            gl = acc[base : base + CLASSES, :]
            hl = acc[base + CLASSES : base + COLS, :]
            whole_g = acc[base : base + CLASSES, BINS - 1 : BINS]
            whole_h = acc[base + CLASSES : base + COLS, BINS - 1 : BINS]
            gr = whole_g - gl
            hr = whole_h - hl
            score = (
                gl * gl / (hl + RIDGE)
                + gr * gr / (hr + RIDGE)
                - whole_g * whole_g / (whole_h + RIDGE)
            )
            gain = jnp.sum(score, axis=0, keepdims=True) * (1.0 / CLASSES)
            for k in range(4):
                at = (n % 2) * 4 + k
                gain_send[n // 2, at : at + 1, :] = gain[:, k * LANES : (k + 1) * LANES]

    def out_copy(pair):
        to = 2 * ((y + 1 + pair // 2) % 4) + pair % 2
        at = out_rs.at[2 * (pair // 2) + core]
        return send(gain_send.at[pair], gain_recv.at[row], out_ss.at[pair], at, to, feat)

    def out_sib_copy():
        at = gain_send.at[NR - 1 - core]
        return send(at, gain_recv.at[row], out_ss.at[NR - 1], out_rs.at[NR - 1], row_at(0, 1), feat)

    gains(0, NODES - CHIP)
    for pair in (2, 3, 0, 1, 4, 5):
        out_copy(pair).start()

    def rest(k, carry):
        accumulate(step_blocks(k), NODES - CHIP, NODES)
        return carry

    lax.fori_loop(2, 6, rest, 0)
    gains(NODES - CHIP, NODES)
    out_sib_copy().start()
    gain_recv[row] = gain_send[NR - 2 + core]

    for d in range(NR - 1):
        dy, other = ROW_ORDER[d]
        arrived(group_tot.at[row_at(4 - dy, other)], gt_rs.at[d])
    totals = group_tot[0]
    for r in range(1, NR):
        totals = totals + group_tot[r]
    total_ref[...] = totals

    for k in range(3):
        for other in range(2):
            came = 2 * ((y + 3 - k) % 4) + other
            arrived(gain_recv.at[came], out_rs.at[2 * k + other])
    arrived(gain_recv.at[row_at(0, 1)], out_rs.at[NR - 1])
    for r in range(NR):
        for n in range(2):
            tile = gain_recv[r, 4 * n : 4 * n + 4, :]
            for side in range(2):
                at = pl.ds(r * FL + side, 4, stride=2)
                gain_ref[n, at, :] = tile[:, side * BINS : (side + 1) * BINS]

    for d in range(1, NF):
        bit_copy(d).wait_send()
    for d in range(NR - 1):
        bin_copy(d).wait_send()
        node_copy(d).wait_send()
        group_tot_copy(d).wait_send()
    for pair in range(6):
        out_copy(pair).wait_send()
    out_sib_copy().wait_send()
    for d in range(1, 4):
        x_copy(d).wait_send()
        chunk_tot_copy(d).wait_send()
    for way in range(2):
        z_copy(way).wait_send()
        z_far_copy(way).wait_send()
    for i in range(4):
        y_copy(0, i).wait_send()
        y_copy(1, i).wait_send()
        y_far_copy(i).wait_send()
        for dy in range(4):
            sib_copy(dy, i).wait_send()


def body(margins, labels, row_bins, parents, split_feature, split_bin, leaf_values):
    vmem = pl.BlockSpec(memory_space=pltpu.VMEM)
    hbm = pl.BlockSpec(memory_space=pltpu.HBM)
    dma = pltpu.SemaphoreType.DMA
    return pl.pallas_call(
        kernel,
        out_shape=(
            jax.ShapeDtypeStruct((2, FD, BINS), F32),
            jax.ShapeDtypeStruct((NODES, COLS), F32),
        ),
        in_specs=[hbm] * 8,
        out_specs=(vmem, vmem),
        scratch_shapes=[
            pltpu.SMEM((PARENTS,), jnp.int32),
            pltpu.SMEM((PARENTS,), jnp.int32),
            pltpu.VMEM((CLASSES, OWN), F32),
            pltpu.VMEM((1, OWN), jnp.int32),
            pltpu.VMEM((FD, GROUP), jnp.int32),
            pltpu.VMEM((KB, LANES), jnp.int32),
            pltpu.VMEM((1, GROUP), jnp.int32),
            pltpu.VMEM((NODES, CLASSES), F32),
            pltpu.VMEM((32, LANES), F32),
            pltpu.VMEM((32, LANES), BF),
            pltpu.VMEM((NF, 32, LANES), BF),
            pltpu.VMEM((NR, KB * FL, LANES), BF),
            pltpu.VMEM((NR, KB * FL, LANES), BF),
            pltpu.VMEM((NR, KB, FL, LANES), F32),
            pltpu.VMEM((NR, KB, LANES), F32),
            pltpu.VMEM((NR, KB, LANES), F32),
            pltpu.VMEM((4, 2, 96, LANES), BF),
            pltpu.VMEM((2, 4, 4, 4, 96, LANES), BF),
            pltpu.VMEM((NODES * COLS, FL * BINS), F32),
            pltpu.VMEM((4, NODES, COLS), F32),
            pltpu.VMEM((NR, NODES, COLS), F32),
            pltpu.VMEM((NR, 8, LANES), F32),
            pltpu.VMEM((NR, 8, LANES), F32),
            dma((8,)),
            dma((NF,)), dma((NF,)), dma((NR,)), dma((NR,)), dma((NR,)), dma((NR,)),
            dma((4,)), dma((4,)), dma((4,)), dma((4,)),
            dma((2, 4)), dma((2, 4)), dma((4,)), dma((4,)), dma((4, 4)), dma((4, 4)),
            dma((NR,)), dma((NR,)),
            dma((4,)), dma((4,)), dma((NR,)), dma((NR,)),
            pltpu.SemaphoreType.REGULAR,
        ],
        compiler_params=pltpu.CompilerParams(
            collective_id=0, has_side_effects=True, vmem_limit_bytes=48 << 20
        ),
    )(
        *(
            pltpu.with_memory_space_constraint(value, pltpu.HBM)
            for value in (
                split_feature,
                split_bin,
                margins.T,
                labels.reshape(1, OWN),
                row_bins,
                parents.reshape(KB, LANES),
                parents.reshape(1, GROUP),
                leaf_values,
            )
        )
    )


def solution(mesh):
    return jax.shard_map(
        body,
        mesh=mesh,
        in_specs=(
            P(("rows", "feat"), None),
            P(("rows", "feat")),
            P("feat", "rows"),
            P("rows"),
            P(),
            P(),
            P(),
        ),
        out_specs=(P("rows", "feat", None), P()),
        check_vma=False,
    )
```
